32 devices in a mesh: member: 4 (over x, core), slab: 8 (over z, y).
Axes of the slice: x: 2, y: 2, z: 4, core: 2. Of those that a mesh axis runs over, the one named last changes fastest.
Arguments:
- ocean_state: float32 [8, 4, 16, 256, 256], P('member', None, 'slab'), may hold values from -6 to 6
- diffusivity: float32 [8, 16, 256, 256], P('member', None, 'slab'), may hold values from 5 to 100
- bottom_drag: float32 [8, 256, 256], P('member', 'slab'), may hold values from 0.5 to 5
- surface_forcing: float32 [2, 3, 256, 256], P(None, None, 'slab', 'member'), may hold values from -6 to 6
- land_sea: int32 [8, 256, 256], P('member'), may hold values 0 or 1
- bottom_level: int32 [8, 256, 256], P('member'), may hold values from 1 to 16
Outputs:
- state_out: float32 [8, 4, 16, 256, 256], P('member', None, 'slab')
The draws below stay inside these ranges and needn't reach their ends.
Inputs may be any that keep to these rules, and one draw needn't show every extreme that they name: `bottom_level`: levels at and below this count are rock.
All inputs are finite; a program needn't handle non-finite values. No bound on the sum of `land_sea` on one device may be relied on, other than what follows from the above.
Results may differ from the reference program's by a relative error of at most 0.0003.
Values sent between devices are 32-bit elements; how exact they have to be, the bound alone decides.
No kernel may reach another device: no remote copies, remote signals or barrier semaphores. Data moves between devices by JAX's collectives and lax.ppermute only.
A program may use at most 128 MiB of HBM per device.

```python
import math
import jax
import jax.numpy as jnp
from jax import lax

MEMBERS = 8
NX = 256
NY = 256
LEVELS = 16
STEPS = 2


def set_ends(array, own_key, low, high):
    shape = array.shape
    place = [jax.random.randint(jax.random.fold_in(own_key, axis), (), 0, shape[axis]) for axis in range(len(shape))]
    array = array.at[tuple(place)].set(low)
    longest = shape.index(max(shape))
    place[longest] = (place[longest] + 1) % shape[longest]
    return array.at[tuple(place)].set(high)


def block_scale(stream_key, dims, cuts, least, high):
    def one(dim, shards_of):
        heights = jax.random.uniform(jax.random.fold_in(jax.random.fold_in(stream_key, 6), dim), (shards_of,), jnp.float32, least / len(cuts), high / len(cuts))
        return jnp.repeat(jnp.exp(heights), dims[dim] // shards_of).reshape((-1,) + (1,) * (len(dims) - dim - 1))

    gain = one(*cuts[0])
    for cut in cuts[1:]:
        gain = gain * one(*cut)
    return gain


def noise(own_key, extent, spread, limit, pieces=(), kind=jnp.bfloat16):
    values = jax.random.normal(own_key, extent, jnp.float32) * spread
    if len(pieces) > 0:
        values = block_scale(own_key, extent, pieces, -0.22, 0.18) * values
    return jnp.clip(values, min=-limit, max=limit).astype(kind)


def setup_inputs(seed: int = 0) -> dict:
    keys = jax.random.split(jax.random.key(seed), 7)
    ocean_state = noise(keys[0], (MEMBERS, 4, LEVELS, NX, NY), 1.0, 6.0, ((0, 4), (2, 8)), jnp.float32)
    diffusivity = jnp.clip(jnp.exp(math.log(100.0) - 2.9957323 * jax.random.uniform(keys[1], (MEMBERS, LEVELS, NX, NY), jnp.float32) ** block_scale(keys[1], (MEMBERS, LEVELS, NX, NY), ((0, 4), (2, 8)), -0.2, 0.2)), 5.0, 100.0)
    bottom_drag = jnp.clip(jnp.exp(math.log(5.0) - 2.3025851 * jax.random.uniform(keys[2], (MEMBERS, NX, NY), jnp.float32) ** block_scale(keys[2], (MEMBERS, NX, NY), ((0, 4), (1, 8)), -0.2, 0.2)), 0.5, 5.0)
    surface_forcing = noise(keys[3], (STEPS, 3, NX, NY), 1.0, 6.0, ((2, 8), (3, 4)), jnp.float32)
    land_sea = set_ends((jax.random.randint(keys[4], (MEMBERS, NX, NY), 0, 4) < 3).astype(jnp.int32), jax.random.fold_in(keys[4], 1), 0, 1)
    bottom_level = set_ends(jax.random.randint(keys[5], (MEMBERS, NX, NY), 1, LEVELS + 1), jax.random.fold_in(keys[5], 1), 1, LEVELS).astype(jnp.int32)
    return {"ocean_state": ocean_state, "diffusivity": diffusivity, "bottom_drag": bottom_drag, "surface_forcing": surface_forcing, "land_sea": land_sea, "bottom_level": bottom_level}


COURANT = 0.2


def wrap_rows(values):
    return jnp.concatenate([values[..., -1:, :], values, values[..., :1, :]], axis=-2)


def wet_cells(land_rows, bottom_rows, level_ids):
    deeper = level_ids[None, :, None, None] < bottom_rows[:, None, :, :]
    ocean = land_rows[:, None, :, :] == 1
    return jnp.where(ocean & deeper, 1.0, 0.0).astype(jnp.float32)


def advect_tracers(tracer_pad, zonal_pad, merid_mid, wet_pad):
    wet_mid = wet_pad[..., 1:-1, :]
    tracer_mid = tracer_pad[..., 1:-1, :]
    face_zonal = 0.5 * (zonal_pad[..., :-1, :] + zonal_pad[..., 1:, :]) * (wet_pad[..., :-1, :] * wet_pad[..., 1:, :])
    flux_zonal = face_zonal * (0.5 * (tracer_pad[..., :-1, :] + tracer_pad[..., 1:, :]))
    spread_zonal = flux_zonal[..., 1:, :] - flux_zonal[..., :-1, :]
    face_merid = 0.5 * (merid_mid[..., :-1] + merid_mid[..., 1:]) * (wet_mid[..., :-1] * wet_mid[..., 1:])
    flux_merid = face_merid * (0.5 * (tracer_mid[..., :-1] + tracer_mid[..., 1:]))
    walls = jnp.zeros(flux_merid.shape[:-1] + (1,), jnp.float32)
    flux_merid = jnp.concatenate([walls, flux_merid, walls], axis=-1)
    spread_merid = flux_merid[..., 1:] - flux_merid[..., :-1]
    return (tracer_mid - COURANT * (spread_zonal + spread_merid)) * wet_mid


def advance(state_pad, wet_pad):
    wet_wide = wet_pad[:, None]
    tracers = advect_tracers(state_pad[:, 0:2], state_pad[:, 2:3], state_pad[:, 3:4, :, 1:-1, :], wet_wide)
    currents = state_pad[:, 2:4, :, 1:-1, :] * wet_wide[..., 1:-1, :]
    return jnp.concatenate([tracers, currents], axis=1)


def mix_columns(columns, diffusivity, bottom_drag, forcing_now, land_rows, bottom_rows, level_ids):
    wet_now = wet_cells(land_rows, bottom_rows, level_ids)
    coupling = diffusivity[:, :-1] * (wet_now[:, :-1] * wet_now[:, 1:])
    edge_zero = jnp.zeros_like(coupling[:, :1])
    rate_above = jnp.concatenate([edge_zero, coupling], axis=1)
    rate_below = jnp.concatenate([coupling, edge_zero], axis=1)
    floor_cells = jnp.where((level_ids[None, :, None, None] == bottom_rows[:, None, :, :] - 1) & (land_rows[:, None, :, :] == 1), 1.0, 0.0).astype(jnp.float32)
    diagonal_base = 1.0 + rate_above + rate_below
    diagonal_drag = diagonal_base + bottom_drag[:, None] * floor_cells
    diagonal_all = jnp.stack([diagonal_base, diagonal_base, diagonal_drag, diagonal_drag], axis=1)
    surface_wet = wet_now[:, 0]
    forcing_terms = jnp.stack([forcing_now[0] * surface_wet, jnp.zeros_like(surface_wet), forcing_now[1] * surface_wet, forcing_now[2] * surface_wet], axis=1)
    right_side = columns.at[:, :, 0].add(forcing_terms)
    lower_band = jnp.moveaxis(-rate_above[:, None], 2, 0)
    upper_band = jnp.moveaxis(-rate_below[:, None], 2, 0)
    diagonal_lev = jnp.moveaxis(diagonal_all, 2, 0)
    right_lev = jnp.moveaxis(right_side, 2, 0)
    start_zero = jnp.zeros(right_lev.shape[1:], jnp.float32)

    def eliminate(previous, level_row):
        prior_upper, prior_right = previous
        lower_row, upper_row, diagonal_row, right_row = level_row
        denominator = diagonal_row - lower_row * prior_upper
        upper_new = upper_row / denominator
        right_new = (right_row - lower_row * prior_right) / denominator
        return (upper_new, right_new), (upper_new, right_new)

    _, (upper_mod, right_mod) = lax.scan(eliminate, (start_zero, start_zero), (lower_band, upper_band, diagonal_lev, right_lev))

    def substitute(next_value, level_row):
        upper_row, right_row = level_row
        value_now = right_row - upper_row * next_value
        return value_now, value_now

    _, solved = lax.scan(substitute, start_zero, (upper_mod, right_mod), reverse=True)
    return jnp.moveaxis(solved, 0, 2)


def reference(ocean_state, diffusivity, bottom_drag, surface_forcing, land_sea, bottom_level):
    level_ids = jnp.arange(LEVELS, dtype=jnp.int32)

    def one_member(bundle):
        member_state, member_diff, member_drag, member_land, member_bottom = bundle
        wet_pad = wrap_rows(wet_cells(member_land, member_bottom, level_ids))
        for step_index in range(STEPS):
            member_state = advance(wrap_rows(member_state), wet_pad)
            member_state = mix_columns(member_state, member_diff, member_drag, surface_forcing[step_index], member_land, member_bottom, level_ids)
        return member_state

    bundles = (ocean_state.reshape(MEMBERS, 1, 4, LEVELS, NX, NY), diffusivity.reshape(MEMBERS, 1, LEVELS, NX, NY), bottom_drag.reshape(MEMBERS, 1, NX, NY), land_sea.reshape(MEMBERS, 1, NX, NY), bottom_level.reshape(MEMBERS, 1, NX, NY))
    finished = lax.map(one_member, bundles)
    return finished.reshape(MEMBERS, 4, LEVELS, NX, NY)
```

```python
import functools

import jax
import jax.numpy as jnp
from jax import lax
from jax.experimental import pallas as pl
from jax.experimental.pallas import tpu as pltpu
from jax.sharding import PartitionSpec as P

STEPS = 2
COURANT = 0.2
F32 = jnp.float32


def shift_next(block, after):
    rows = block.shape[0]
    row_ids = lax.broadcasted_iota(jnp.int32, block.shape, 0)
    return jnp.where(row_ids == rows - 1, after, pltpu.roll(block, rows - 1, 0))


def shift_prev(block, before):
    row_ids = lax.broadcasted_iota(jnp.int32, block.shape, 0)
    return jnp.where(row_ids == 0, before, pltpu.roll(block, 1, 0))


def lane_next(block):
    return pltpu.roll(block, block.shape[1] - 1, 1)


def lane_prev(block):
    return pltpu.roll(block, 1, 1)


def advect_tile(tracers, zonal, merid, counts, level):
    cell_n, zonal_n, zonal_first_n, merid_n = counts
    u, u_before, u_after = zonal
    face_u = jnp.where(level < zonal_n, 0.25 * (u + shift_next(u, u_after)), 0.0)
    first_u = jnp.where(level < zonal_first_n, 0.25 * (u_before + u[0:1]), 0.0)
    face_v = jnp.where(level < merid_n, 0.25 * (merid + lane_next(merid)), 0.0)
    out = []
    for c, c_before, c_after in tracers:
        flux_x = face_u * (c + shift_next(c, c_after))
        first_x = first_u * (c_before + c[0:1])
        flux_y = face_v * (c + lane_next(c))
        spread = (flux_x - shift_prev(flux_x, first_x)) + (flux_y - lane_prev(flux_y))
        out.append(jnp.where(level < cell_n, c - COURANT * spread, 0.0))
    return out


def advect_kernel(groups, rows, levels_own, scal, state, cell_n, zonal_n, merid_n, *outs):
    level_here = pl.program_id(0)
    nx = state.shape[3]
    group = scal[0]
    level = scal[2] + level_here
    for part in range(groups):
        for tile in range(2):
            row0 = (tile * groups + (group ^ part)) * rows
            before = pl.multiple_of(lax.rem(row0 + nx - 8, nx), 8)
            after = pl.multiple_of(lax.rem(row0 + rows, nx), 8)
            here = pl.multiple_of(row0, 8)

            def whole(field):
                return (
                    state[0, field, 0, pl.ds(here, rows), :],
                    state[0, field, 0, pl.ds(before, 8), :][7:8],
                    state[0, field, 0, pl.ds(after, 8), :][0:1],
                )

            counts = (
                cell_n[0, pl.ds(here, rows), :],
                zonal_n[0, pl.ds(here, rows), :],
                zonal_n[0, pl.ds(before, 8), :][7:8],
                merid_n[0, pl.ds(here, rows), :],
            )
            merid = state[0, 3, 0, pl.ds(here, rows), :]
            moved = advect_tile([whole(0), whole(1)], whole(2), merid, counts, level)
            for field in range(2):
                outs[part][0, field, 0, tile] = moved[field]


def factor_kernel(half_levels, scal, own, got, own_drag, cell_n, rate, inv_t, inv_v, mid):
    half = scal[1]
    tile = pl.program_id(1)
    top = half == 0
    start = half * (half_levels - 1)
    is_own = tile == half
    count = cell_n[0, 0]
    shape = count.shape
    drag = jnp.where(is_own, own_drag[0], got[0, half_levels])
    prev = jnp.zeros(shape, F32)
    c_t = prev
    c_v = prev
    for e in range(half_levels):
        spot = jnp.where(top, e, half_levels - 1 - e)
        deeper = jnp.where(top, e + 1, 2 * half_levels - 1 - e)
        level = jnp.where(top, e, 2 * half_levels - 1 - e)
        diff = jnp.where(is_own, own[0, start + spot], got[0, spot])
        r = jnp.where(deeper < count, diff, 0.0)
        base = 1.0 + r
        den_t = base + prev * (1.0 - c_t)
        den_v = base + prev * (1.0 - c_v) + jnp.where(level == count - 1, drag, 0.0)
        i_t = 1.0 / den_t
        i_v = 1.0 / den_v
        rate[0, 0, e] = r
        inv_t[0, 0, e] = i_t
        inv_v[0, 0, e] = i_v
        c_t = r * i_t
        c_v = r * i_v
        prev = r
    mid[0, 0, 0] = c_t
    mid[0, 0, 1] = c_v


def sweep(rhs, rate, inv, store):
    half_levels = rate.shape[2]
    carry = [None, None]
    before = None
    for e in range(half_levels):
        inverse = inv[0, 0, e]
        for f in range(2):
            value = rhs(e, f)
            if e > 0:
                value = value + before * carry[f]
            carry[f] = value * inverse
            store(e, f, carry[f])
        before = rate[0, 0, e]
    return carry


def back(d_ref, other, rate, inv, mid, mid_other, kind, store):
    half_levels = rate.shape[2]
    last = half_levels - 1
    c_own = mid[0, 0, kind]
    c_oth = mid_other[0, 0, kind]
    scale = 1.0 / (1.0 - c_own * c_oth)
    value = [(d_ref[0, 0, f, last] + c_own * other[0, 0, f]) * scale for f in range(2)]
    for f in range(2):
        store(last, f, value[f])
    for e in range(last - 1, -1, -1):
        c = rate[0, 0, e] * inv[0, 0, e]
        for f in range(2):
            value[f] = d_ref[0, 0, f, e] + c * value[f]
            store(e, f, value[f])


def forced(forcing, count, force_ids, f):
    if force_ids[f] is None:
        return 0.0
    return jnp.where(count > 0, forcing[0, force_ids[f], 0], 0.0)


def first_kernel(groups, levels_own, force_ids, masked, scal, *refs):
    chunks = refs[:groups]
    rate, inv, cell_n, forcing, d_ref, mid_ref, buf = refs[groups:]
    count = cell_n[0, 0]
    for part in range(groups):
        for lev in range(levels_own):
            at = 3 + part * levels_own + lev
            slot = scal[at]
            level = scal[at + groups * levels_own]
            for f in range(2):
                value = chunks[part][0, f, lev, 0]
                buf[f, slot] = value if masked else jnp.where(level < count, value, 0.0)

    def rhs(e, f):
        value = buf[f, e]
        return value + forced(forcing, count, force_ids, f) if e == 0 else value

    def store(e, f, value):
        d_ref[0, 0, f, e] = value

    carry = sweep(rhs, rate, inv, store)
    for f in range(2):
        mid_ref[0, 0, f] = carry[f]


def middle_v_kernel(scal, d_ref, other, rate, inv, mid, mid_other, cell_n, forcing, x_ref, top_ref, end_ref, d2_ref, mid2_ref):
    rows = x_ref.shape[4]

    def keep(e, f, value):
        x_ref[0, 0, f, e] = value
        if f == 0:
            top_ref[0, 0, pl.ds(e, 1), :] = value[0:1]
            end_ref[0, 0, pl.ds(e, 1), :] = value[rows - 1 : rows]

    back(d_ref, other, rate, inv, mid, mid_other, 1, keep)
    count = cell_n[0, 0]

    def rhs(e, f):
        value = x_ref[0, 0, f, e]
        return value + forced(forcing, count, (1, 2), f) if e == 0 else value

    def store(e, f, value):
        d2_ref[0, 0, f, e] = value

    carry = sweep(rhs, rate, inv, store)
    for f in range(2):
        mid2_ref[0, 0, f] = carry[f]


def middle_t_kernel(scal, d_ref, other, rate, inv, mid, mid_other, x_ref, top_ref, end_ref):
    rows = x_ref.shape[4]

    def keep(e, f, value):
        x_ref[0, 0, f, e] = value
        top_ref[0, 0, f, pl.ds(e, 1), :] = value[0:1]
        end_ref[0, 0, f, pl.ds(e, 1), :] = value[rows - 1 : rows]

    back(d_ref, other, rate, inv, mid, mid_other, 0, keep)


def second_t_kernel(scal, x_ref, v_ref, t_before, t_after, u_before, u_after, rate, inv, cell_n, zonal_n, first_n, merid_n, forcing, d_ref, mid_ref, buf):
    half_levels = rate.shape[2]
    top = scal[1] == 0
    count = cell_n[0, 0]
    counts = (count, zonal_n[0, 0], first_n[0, 0], merid_n[0, 0])
    for e in range(half_levels):
        level = jnp.where(top, e, 2 * half_levels - 1 - e)
        tracers = [
            (x_ref[0, 0, f, e], t_before[0, 0, f, e : e + 1, :], t_after[0, 0, f, e : e + 1, :]) for f in range(2)
        ]
        zonal = (v_ref[0, 0, 0, e], u_before[0, 0, e : e + 1, :], u_after[0, 0, e : e + 1, :])
        moved = advect_tile(tracers, zonal, v_ref[0, 0, 1, e], counts, level)
        for f in range(2):
            buf[f, e] = moved[f]

    def rhs(e, f):
        value = buf[f, e]
        return value + forced(forcing, count, (0, None), f) if e == 0 else value

    def store(e, f, value):
        d_ref[0, 0, f, e] = value

    carry = sweep(rhs, rate, inv, store)
    for f in range(2):
        mid_ref[0, 0, f] = carry[f]


def last_kernel(groups, levels_own, kind, scal, d_ref, other, rate, inv, mid, mid_other, *refs):
    outs = refs[:groups]
    buf = refs[groups]

    def keep(e, f, value):
        buf[f, e] = value

    back(d_ref, other, rate, inv, mid, mid_other, kind, keep)
    for part in range(groups):
        for lev in range(levels_own):
            slot = scal[3 + part * levels_own + lev]
            for f in range(2):
                outs[part][0, f, lev, 0] = buf[f, slot]


def place_kernel(groups, member, fields, aliased, scal, *refs):
    chunks = refs[:groups]
    out, sem = refs[groups + (1 if aliased else 0) :]
    copies = []
    for part in range(groups):
        place = scal[0] ^ part
        members = chunks[part].shape[0]
        copies.append(
            pltpu.make_async_copy(
                chunks[part],
                out.at[pl.ds(member, members), pl.ds(fields, 2), :, :, place],
                sem.at[part],
            )
        )
    for copy in copies:
        copy.start()
    for copy in copies:
        copy.wait()


VMEM_LIMIT = 40 * 1024 * 1024


def call(kernel, name, scal, grid, inputs, outputs, scratch=(), aliases=None, cost=None):
    def spec(block, index):
        if block is None:
            return pl.BlockSpec(memory_space=pl.ANY)
        return pl.BlockSpec(block, index)

    bytes_moved = sum(a.size * 4 for a, b, _ in inputs if b is not None)
    for s, b, _ in outputs:
        size = 4
        for dim in s:
            size *= dim
        bytes_moved += size
    return pl.pallas_call(
        kernel,
        grid_spec=pltpu.PrefetchScalarGridSpec(
            num_scalar_prefetch=1,
            grid=grid,
            in_specs=[spec(b, i) for _, b, i in inputs],
            out_specs=[spec(b, i) for _, b, i in outputs],
            scratch_shapes=list(scratch),
        ),
        out_shape=[jax.ShapeDtypeStruct(s, F32) for s, _, _ in outputs],
        input_output_aliases=aliases or {},
        compiler_params=pltpu.CompilerParams(vmem_limit_bytes=VMEM_LIMIT),
        cost_estimate=pl.CostEstimate(flops=bytes_moved * 4, bytes_accessed=bytes_moved, transcendentals=0),
        name=name,
    )(scal, *[a for a, _, _ in inputs])


def per_device(slabs, ocean_state, diffusivity, bottom_drag, surface_forcing, land_sea, bottom_level):
    members, _, own, nx, ny = ocean_state.shape
    groups = slabs // 2
    rows = nx // slabs
    levels = diffusivity.shape[1]
    half_levels = levels // 2
    slab = lax.axis_index("slab")
    half = slab // groups
    group = slab % groups
    partner = [(i, (i + groups) % slabs) for i in range(slabs)]

    def swap(values):
        return lax.ppermute(values, "slab", partner)

    def cross(values, part):
        return lax.ppermute(values, "slab", [(i, (i // groups) * groups + ((i % groups) ^ part)) for i in range(slabs)])

    to_next = [(i, (i // groups) * groups + (i % groups + 1) % groups) for i in range(slabs)]
    to_prev = [(b, a) for a, b in to_next]

    parts = jnp.arange(groups, dtype=jnp.int32)
    local = ((group ^ parts)[:, None] * own + jnp.arange(own, dtype=jnp.int32)[None, :]).reshape(-1)
    slots = jnp.where(half == 0, local, half_levels - 1 - local)
    scal = jnp.concatenate(
        [
            jnp.stack([group, half, slab * own, ]).astype(jnp.int32),
            slots,
            half * half_levels + local,
        ]
    ).astype(jnp.int32)

    view = ocean_state.reshape(members, 4, own, 2, groups, rows, ny)
    v_send = [
        lax.dynamic_index_in_dim(view[:, 2:4], group ^ part, 4, keepdims=False) for part in range(groups)
    ]
    v_got = [v_send[0]] + [cross(v_send[part], part) for part in range(1, groups)]

    give = jnp.concatenate(
        [
            lax.dynamic_slice_in_dim(diffusivity, (1 - half) * (half_levels - 1), half_levels, 1),
            bottom_drag[:, None],
        ],
        axis=1,
    )
    got = swap(give)

    f_got = swap(surface_forcing)
    f_tiles = jnp.where(half == 0, jnp.stack([surface_forcing, f_got], axis=2), 0.0)
    forcing = lax.all_gather(f_tiles, "member", axis=4, tiled=True)

    cell_n = jnp.where(land_sea == 1, bottom_level, 0)
    zonal_n = jnp.minimum(cell_n, jnp.roll(cell_n, -1, axis=1))
    merid_n = jnp.minimum(cell_n, jnp.concatenate([cell_n[:, :, 1:], jnp.zeros_like(cell_n[:, :, :1])], axis=2))

    def tiles(values):
        return lax.dynamic_index_in_dim(values.reshape(members, 2, groups, rows, ny), group, 2, keepdims=False)

    cell_t = tiles(cell_n)
    zonal_t = tiles(zonal_n)
    merid_t = tiles(merid_n)
    first_t = tiles(jnp.roll(zonal_n, 1, axis=1))[:, :, :1]

    chunk_shape = (1, 2, own, 2, rows, ny)

    def advected(m):
        return call(
            functools.partial(advect_kernel, groups, rows, own),
            "advect",
            scal,
            (own,),
            [
                (ocean_state, (1, 4, 1, nx, ny), lambda l, s: (m, 0, l, 0, 0)),
                (cell_n, (1, nx, ny), lambda l, s: (m, 0, 0)),
                (zonal_n, (1, nx, ny), lambda l, s: (m, 0, 0)),
                (merid_n, (1, nx, ny), lambda l, s: (m, 0, 0)),
            ],
            [(chunk_shape, (1, 2, 1, 2, rows, ny), lambda l, s: (0, 0, l, 0, 0, 0))] * groups,
        )

    t_send = [advected(m) for m in range(members)]
    t_got = [[t_send[m][0]] + [cross(t_send[m][part], part) for part in range(1, groups)] for m in range(members)]

    col_shape = (members, 2, half_levels, rows, ny)
    col_block = (1, 1, half_levels, rows, ny)
    rate, inv_t, inv_v, mid = call(
        functools.partial(factor_kernel, half_levels),
        "factor",
        scal,
        (members, 2),
        [
            (diffusivity, (1, levels, rows, ny), lambda m, t, s: (m, 0, 0, 0)),
            (got, (1, half_levels + 1, rows, ny), lambda m, t, s: (m, 0, 0, 0)),
            (bottom_drag, (1, rows, ny), lambda m, t, s: (m, 0, 0)),
            (cell_t, (1, 1, rows, ny), lambda m, t, s: (m, t, 0, 0)),
        ],
        [
            (col_shape, col_block, lambda m, t, s: (m, t, 0, 0, 0)),
            (col_shape, col_block, lambda m, t, s: (m, t, 0, 0, 0)),
            (col_shape, col_block, lambda m, t, s: (m, t, 0, 0, 0)),
            ((members, 2, 2, rows, ny), (1, 1, 2, rows, ny), lambda m, t, s: (m, t, 0, 0, 0)),
        ],
    )
    mid_other = swap(mid)

    state_block = (1, 1, 2, half_levels, rows, ny)
    pair_block = (1, 1, 2, rows, ny)

    def at(m0):
        def mine(extra):
            return lambda m, t, s: (m, t) + (0,) * extra

        def shared(extra):
            return lambda m, t, s: (m + m0, t) + (0,) * extra

        return mine, shared

    def first(chunks, m0, count, inv, force_ids, masked):
        mine, shared = at(m0)
        return call(
            functools.partial(first_kernel, groups, own, force_ids, masked),
            "first",
            scal,
            (count, 2),
            [(c, (1, 2, own, 1, rows, ny), lambda m, t, s: (m, 0, 0, t, 0, 0)) for c in chunks]
            + [
                (rate, col_block, shared(3)),
                (inv, col_block, shared(3)),
                (cell_t, (1, 1, rows, ny), shared(2)),
                (forcing, (1, 3, 1, rows, ny), lambda m, t, s: (0, 0, t, 0, 0)),
            ],
            [
                ((count, 2, 2, half_levels, rows, ny), state_block, mine(4)),
                ((count, 2, 2, rows, ny), pair_block, mine(3)),
            ],
            [pltpu.VMEM((2, half_levels, rows, ny), F32)],
        )

    def last(d, other, m0, count, inv, kind):
        mine, shared = at(m0)
        return call(
            functools.partial(last_kernel, groups, own, kind),
            "last",
            scal,
            (count, 2),
            [
                (d, state_block, mine(4)),
                (other, pair_block, mine(3)),
                (rate, col_block, shared(3)),
                (inv, col_block, shared(3)),
                (mid, pair_block, shared(3)),
                (mid_other, pair_block, shared(3)),
            ],
            [((count, 2, own, 2, rows, ny), (1, 2, own, 1, rows, ny), lambda m, t, s: (m, 0, 0, t, 0, 0))] * groups,
            [pltpu.VMEM((2, half_levels, rows, ny), F32)],
        )

    mine, shared = at(0)
    d_v, dm_v = first(v_got, 0, members, inv_v, (1, 2), False)
    dm_v_other = swap(dm_v)
    x_v, u_top, u_end, d2_v, dm2_v = call(
        middle_v_kernel,
        "middle_v",
        scal,
        (members, 2),
        [
            (d_v, state_block, mine(4)),
            (dm_v_other, pair_block, mine(3)),
            (rate, col_block, shared(3)),
            (inv_v, col_block, shared(3)),
            (mid, pair_block, shared(3)),
            (mid_other, pair_block, shared(3)),
            (cell_t, (1, 1, rows, ny), shared(2)),
            (forcing, (1, 3, 1, rows, ny), lambda m, t, s: (1, 0, t, 0, 0)),
        ],
        [
            ((members, 2, 2, half_levels, rows, ny), state_block, mine(4)),
            ((members, 2, half_levels, ny), (1, 1, half_levels, ny), mine(2)),
            ((members, 2, half_levels, ny), (1, 1, half_levels, ny), mine(2)),
            ((members, 2, 2, half_levels, rows, ny), state_block, mine(4)),
            ((members, 2, 2, rows, ny), pair_block, mine(3)),
        ],
    )
    dm2_v_other = swap(dm2_v)
    u_before = lax.ppermute(u_end, "slab", to_next)
    u_after = lax.ppermute(u_top, "slab", to_prev)
    out_v = last(d2_v, dm2_v_other, 0, members, inv_v, 1)
    back_v = [out_v[0]] + [cross(out_v[part], part) for part in range(1, groups)]

    back_t = []
    for m in range(members):
        mine, shared = at(m)
        d_t, dm_t = first(t_got[m], m, 1, inv_t, (0, None), True)
        dm_t_other = swap(dm_t)
        x_t, t_top, t_end = call(
            middle_t_kernel,
            "middle_t",
            scal,
            (1, 2),
            [
                (d_t, state_block, mine(4)),
                (dm_t_other, pair_block, mine(3)),
                (rate, col_block, shared(3)),
                (inv_t, col_block, shared(3)),
                (mid, pair_block, shared(3)),
                (mid_other, pair_block, shared(3)),
            ],
            [
                ((1, 2, 2, half_levels, rows, ny), state_block, mine(4)),
                ((1, 2, 2, half_levels, ny), (1, 1, 2, half_levels, ny), mine(3)),
                ((1, 2, 2, half_levels, ny), (1, 1, 2, half_levels, ny), mine(3)),
            ],
        )
        t_before = lax.ppermute(t_end, "slab", to_next)
        t_after = lax.ppermute(t_top, "slab", to_prev)

        def from_before(extra, m0):
            return lambda i, t, s: (i + m0, t ^ jnp.where(s[0] == 0, 1, 0)) + (0,) * extra

        def from_after(extra, m0):
            return lambda i, t, s: (i + m0, t ^ jnp.where(s[0] == groups - 1, 1, 0)) + (0,) * extra

        d2_t, dm2_t = call(
            second_t_kernel,
            "second_t",
            scal,
            (1, 2),
            [
                (x_t, state_block, mine(4)),
                (x_v, state_block, shared(4)),
                (t_before, (1, 1, 2, half_levels, ny), from_before(3, 0)),
                (t_after, (1, 1, 2, half_levels, ny), from_after(3, 0)),
                (u_before, (1, 1, half_levels, ny), from_before(2, m)),
                (u_after, (1, 1, half_levels, ny), from_after(2, m)),
                (rate, col_block, shared(3)),
                (inv_t, col_block, shared(3)),
                (cell_t, (1, 1, rows, ny), shared(2)),
                (zonal_t, (1, 1, rows, ny), shared(2)),
                (first_t, (1, 1, 1, ny), shared(2)),
                (merid_t, (1, 1, rows, ny), shared(2)),
                (forcing, (1, 3, 1, rows, ny), lambda i, t, s: (1, 0, t, 0, 0)),
            ],
            [
                ((1, 2, 2, half_levels, rows, ny), state_block, mine(4)),
                ((1, 2, 2, rows, ny), pair_block, mine(3)),
            ],
            [pltpu.VMEM((2, half_levels, rows, ny), F32)],
        )
        out_t = last(d2_t, swap(dm2_t), m, 1, inv_t, 0)
        back_t.append([out_t[0]] + [cross(out_t[part], part) for part in range(1, groups)])

    whole = view.shape
    sems = [pltpu.SemaphoreType.DMA((groups,))]
    (result,) = call(
        functools.partial(place_kernel, groups, 0, 2, False),
        "place_v",
        scal,
        (),
        [(c, None, None) for c in back_v],
        [(whole, None, None)],
        sems,
    )
    for m in range(members):
        (result,) = call(
            functools.partial(place_kernel, groups, m, 0, True),
            "place_t",
            scal,
            (),
            [(c, None, None) for c in back_t[m]] + [(result, None, None)],
            [(whole, None, None)],
            sems,
            {groups + 1: 0},
        )
    return result.reshape(ocean_state.shape)


def solution(mesh):
    placed = (
        P("member", None, "slab", None, None),
        P("member", None, "slab", None),
        P("member", "slab", None),
        P(None, None, "slab", "member"),
        P("member", None, None),
        P("member", None, None),
    )
    return jax.shard_map(
        functools.partial(per_device, mesh.shape["slab"]),
        mesh=mesh,
        in_specs=placed,
        out_specs=P("member", None, "slab", None, None),
        check_vma=False,
    )
```

```python
import functools

import jax
import jax.numpy as jnp
from jax import lax
from jax.experimental import pallas as pl
from jax.experimental.pallas import tpu as pltpu
from jax.sharding import PartitionSpec as P

STEPS = 2
COURANT = 0.2
F32 = jnp.float32


def shift_next(block, after):
    rows = block.shape[0]
    row_ids = lax.broadcasted_iota(jnp.int32, block.shape, 0)
    return jnp.where(row_ids == rows - 1, after, pltpu.roll(block, rows - 1, 0))


def shift_prev(block, before):
    row_ids = lax.broadcasted_iota(jnp.int32, block.shape, 0)
    return jnp.where(row_ids == 0, before, pltpu.roll(block, 1, 0))


def lane_next(block):
    return pltpu.roll(block, block.shape[1] - 1, 1)


def lane_prev(block):
    return pltpu.roll(block, 1, 1)


def advect_tile(tracers, zonal, merid, counts, level):
    cell_n, zonal_n, zonal_first_n, merid_n = counts
    u, u_before, u_after = zonal
    face_u = jnp.where(level < zonal_n, 0.25 * (u + shift_next(u, u_after)), 0.0)
    first_u = jnp.where(level < zonal_first_n, 0.25 * (u_before + u[0:1]), 0.0)
    face_v = jnp.where(level < merid_n, 0.25 * (merid + lane_next(merid)), 0.0)
    out = []
    for c, c_before, c_after in tracers:
        flux_x = face_u * (c + shift_next(c, c_after))
        first_x = first_u * (c_before + c[0:1])
        flux_y = face_v * (c + lane_next(c))
        spread = (flux_x - shift_prev(flux_x, first_x)) + (flux_y - lane_prev(flux_y))
        out.append(jnp.where(level < cell_n, c - COURANT * spread, 0.0))
    return out


def advect_kernel(groups, rows, scal, state, cell_n, zonal_n, merid_n, *outs):
    nx = state.shape[3]
    level = scal[2] + pl.program_id(1)
    for part in range(groups):
        for tile in range(2):
            row0 = (tile * groups + (scal[0] ^ part)) * rows
            before = pl.multiple_of(lax.rem(row0 + nx - 8, nx), 8)
            after = pl.multiple_of(lax.rem(row0 + rows, nx), 8)
            here = pl.multiple_of(row0, 8)

            def whole(field):
                return (
                    state[0, field, 0, pl.ds(here, rows), :],
                    state[0, field, 0, pl.ds(before, 8), :][7:8],
                    state[0, field, 0, pl.ds(after, 8), :][0:1],
                )

            counts = (
                cell_n[0, pl.ds(here, rows), :],
                zonal_n[0, pl.ds(here, rows), :],
                zonal_n[0, pl.ds(before, 8), :][7:8],
                merid_n[0, pl.ds(here, rows), :],
            )
            merid = state[0, 3, 0, pl.ds(here, rows), :]
            moved = advect_tile([whole(0), whole(1)], whole(2), merid, counts, level)
            for field in range(2):
                outs[part][0, field, 0, tile] = moved[field]


def split_kernel(groups, rows, scal, state, *outs):
    for part in range(groups):
        for tile in range(2):
            here = pl.multiple_of((tile * groups + (scal[0] ^ part)) * rows, 8)
            for field in range(2):
                outs[part][0, field, 0, tile] = state[0, field, 0, pl.ds(here, rows), :]


def give_kernel(half_levels, scal, own, drag, land, bottom, out, mid_other):
    half = scal[1]
    count = jnp.where(land[0] == 1, bottom[0], 0)
    shape = count.shape
    for e in range(half_levels):
        out[0, e] = own[0, (1 - half) * (half_levels - 1) + e]
    out[0, half_levels] = drag[0]

    def ends(which):
        top = which == 0
        prev = jnp.zeros(shape, F32)
        c_t = prev
        c_v = prev
        for e in range(half_levels):
            upper = jnp.where(top, e, 2 * half_levels - 2 - e)
            level = jnp.where(top, e, 2 * half_levels - 1 - e)
            r = jnp.where(upper + 1 < count, own[0, upper], 0.0)
            base = 1.0 + r
            c_v = r / (base + prev * (1.0 - c_v) + jnp.where(level == count - 1, drag[0], 0.0))
            c_t = r / (base + prev * (1.0 - c_t))
            prev = r
        return c_t, c_v

    mine = ends(half)
    others = ends(1 - half)
    for kind in range(2):
        out[0, half_levels + 1 + kind] = mine[kind]
        mid_other[0, kind] = others[kind]


def factor_kernel(half_levels, scal, own, got, own_drag, own_other, cell_n, rate, inv_t, inv_v, mid, mid_other):
    half = scal[1]
    tile = pl.program_id(1)
    top = half == 0
    start = half * (half_levels - 1)
    is_own = tile == half
    count = cell_n[0, 0]
    shape = count.shape
    drag = jnp.where(is_own, own_drag[0], got[0, half_levels])
    prev = jnp.zeros(shape, F32)
    c_t = prev
    c_v = prev
    for e in range(half_levels):
        spot = jnp.where(top, e, half_levels - 1 - e)
        deeper = jnp.where(top, e + 1, 2 * half_levels - 1 - e)
        level = jnp.where(top, e, 2 * half_levels - 1 - e)
        diff = jnp.where(is_own, own[0, start + spot], got[0, spot])
        r = jnp.where(deeper < count, diff, 0.0)
        base = 1.0 + r
        den_t = base + prev * (1.0 - c_t)
        den_v = base + prev * (1.0 - c_v) + jnp.where(level == count - 1, drag, 0.0)
        i_t = 1.0 / den_t
        i_v = 1.0 / den_v
        rate[0, 0, e] = r
        inv_t[0, 0, e] = i_t
        inv_v[0, 0, e] = i_v
        c_t = r * i_t
        c_v = r * i_v
        prev = r
    mid[0, 0, 0] = c_t
    mid[0, 0, 1] = c_v
    for kind in range(2):
        mid_other[0, 0, kind] = jnp.where(is_own, own_other[0, kind], got[0, half_levels + 1 + kind])


def sweep(rhs, rate, inv, store):
    half_levels = rate.shape[2]
    carry = [None, None]
    before = None
    for e in range(half_levels):
        inverse = inv[0, 0, e]
        for f in range(2):
            value = rhs(e, f)
            if e > 0:
                value = value + before * carry[f]
            carry[f] = value * inverse
            store(e, f, carry[f])
        before = rate[0, 0, e]
    return carry


def back(d_ref, other, rate, inv, mid, mid_other, kind, store):
    half_levels = rate.shape[2]
    last = half_levels - 1
    c_own = mid[0, 0, kind]
    c_oth = mid_other[0, 0, kind]
    scale = 1.0 / (1.0 - c_own * c_oth)
    value = [(d_ref[0, 0, f, last] + c_own * other[0, 0, f]) * scale for f in range(2)]
    for f in range(2):
        store(last, f, value[f])
    for e in range(last - 1, -1, -1):
        c = rate[0, 0, e] * inv[0, 0, e]
        for f in range(2):
            value[f] = d_ref[0, 0, f, e] + c * value[f]
            store(e, f, value[f])


def forced(forcing, count, force_ids, f):
    if force_ids[f] is None:
        return 0.0
    return jnp.where(count > 0, forcing[0, force_ids[f], 0], 0.0)


def slot_of(scal, part, lev, levels_own, half_levels):
    spot = (scal[0] ^ part) * levels_own + lev
    return jnp.where(scal[1] == 0, spot, half_levels - 1 - spot)


def first_kernel(groups, levels_own, force_ids, masked, scal, *refs):
    chunks = refs[:groups]
    rate, inv, cell_n, forcing, d_ref, mid_ref, buf = refs[groups:]
    half_levels = rate.shape[2]
    count = cell_n[0, 0]
    for part in range(groups):
        for lev in range(levels_own):
            slot = slot_of(scal, part, lev, levels_own, half_levels)
            level = scal[1] * half_levels + (scal[0] ^ part) * levels_own + lev
            for f in range(2):
                value = chunks[part][0, f, lev, 0]
                buf[f, slot] = value if masked else jnp.where(level < count, value, 0.0)

    def rhs(e, f):
        value = buf[f, e]
        return value + forced(forcing, count, force_ids, f) if e == 0 else value

    def store(e, f, value):
        d_ref[0, 0, f, e] = value

    carry = sweep(rhs, rate, inv, store)
    for f in range(2):
        mid_ref[0, 0, f] = carry[f]


def middle_v_kernel(scal, d_ref, other, rate, inv, mid, mid_other, cell_n, forcing, x_ref, top_ref, end_ref, d2_ref, mid2_ref):
    rows = x_ref.shape[4]

    def keep(e, f, value):
        x_ref[0, 0, f, e] = value
        if f == 0:
            top_ref[0, 0, pl.ds(e, 1), :] = value[0:1]
            end_ref[0, 0, pl.ds(e, 1), :] = value[rows - 1 : rows]

    back(d_ref, other, rate, inv, mid, mid_other, 1, keep)
    count = cell_n[0, 0]

    def rhs(e, f):
        value = x_ref[0, 0, f, e]
        return value + forced(forcing, count, (1, 2), f) if e == 0 else value

    def store(e, f, value):
        d2_ref[0, 0, f, e] = value

    carry = sweep(rhs, rate, inv, store)
    for f in range(2):
        mid2_ref[0, 0, f] = carry[f]


def middle_t_kernel(scal, d_ref, other, rate, inv, mid, mid_other, x_ref, top_ref, end_ref):
    rows = x_ref.shape[4]

    def keep(e, f, value):
        x_ref[0, 0, f, e] = value
        top_ref[0, 0, f, pl.ds(e, 1), :] = value[0:1]
        end_ref[0, 0, f, pl.ds(e, 1), :] = value[rows - 1 : rows]

    back(d_ref, other, rate, inv, mid, mid_other, 0, keep)


def second_t_kernel(scal, x_ref, v_ref, t_before, t_after, u_before, u_after, rate, inv, cell_n, zonal_n, first_n, merid_n, forcing, d_ref, mid_ref, buf):
    half_levels = rate.shape[2]
    top = scal[1] == 0
    count = cell_n[0, 0]
    counts = (count, zonal_n[0, 0], first_n[0, 0], merid_n[0, 0])
    for e in range(half_levels):
        level = jnp.where(top, e, 2 * half_levels - 1 - e)
        tracers = [
            (x_ref[0, 0, f, e], t_before[0, 0, f, e : e + 1, :], t_after[0, 0, f, e : e + 1, :]) for f in range(2)
        ]
        zonal = (v_ref[0, 0, 0, e], u_before[0, 0, e : e + 1, :], u_after[0, 0, e : e + 1, :])
        moved = advect_tile(tracers, zonal, v_ref[0, 0, 1, e], counts, level)
        for f in range(2):
            buf[f, e] = moved[f]

    def rhs(e, f):
        value = buf[f, e]
        return value + forced(forcing, count, (0, None), f) if e == 0 else value

    def store(e, f, value):
        d_ref[0, 0, f, e] = value

    carry = sweep(rhs, rate, inv, store)
    for f in range(2):
        mid_ref[0, 0, f] = carry[f]


def last_kernel(groups, levels_own, kind, scal, d_ref, other, rate, inv, mid, mid_other, *refs):
    outs, buf = refs[:groups], refs[groups]
    half_levels = rate.shape[2]

    def keep(e, f, value):
        buf[f, e] = value

    back(d_ref, other, rate, inv, mid, mid_other, kind, keep)
    for part in range(groups):
        for lev in range(levels_own):
            slot = slot_of(scal, part, lev, levels_own, half_levels)
            for f in range(2):
                outs[part][0, f, lev, 0] = buf[f, slot]


def place_kernel(groups, member, fields, aliased, scal, *refs):
    chunks = refs[:groups]
    out, sem = refs[groups + (1 if aliased else 0) :]
    copies = []
    for part in range(groups):
        members = chunks[part].shape[0]
        copies.append(
            pltpu.make_async_copy(
                chunks[part],
                out.at[pl.ds(member, members), pl.ds(fields, 2), :, :, scal[0] ^ part],
                sem.at[part],
            )
        )
    for copy in copies:
        copy.start()
    for copy in copies:
        copy.wait()


def pick(values, which):
    out = values[0]
    for index in range(1, len(values)):
        out = jnp.where(which == index, values[index], out)
    return out


def call(kernel, name, scal, grid, inputs, outputs, scratch=(), aliases=None, limit=40):
    def spec(block, index):
        if block is None:
            return pl.BlockSpec(memory_space=pl.ANY)
        if block == "VMEM":
            return pl.BlockSpec(memory_space=pltpu.VMEM)
        return pl.BlockSpec(block, index)

    bytes_moved = sum(a.size * 4 for a, b, _ in inputs if b is not None)
    for s, b, _ in outputs:
        size = 4
        for dim in s:
            size *= dim
        bytes_moved += size
    return pl.pallas_call(
        kernel,
        grid_spec=pltpu.PrefetchScalarGridSpec(
            num_scalar_prefetch=1,
            grid=grid,
            in_specs=[spec(b, i) for _, b, i in inputs],
            out_specs=[spec(b, i) for _, b, i in outputs],
            scratch_shapes=list(scratch),
        ),
        out_shape=[jax.ShapeDtypeStruct(s, F32) for s, _, _ in outputs],
        input_output_aliases=aliases or {},
        compiler_params=pltpu.CompilerParams(vmem_limit_bytes=limit * 1024 * 1024),
        cost_estimate=pl.CostEstimate(flops=0, bytes_accessed=bytes_moved // 1024, transcendentals=0),
        name=name,
    )(scal, *[a for a, _, _ in inputs])


def per_device(slabs, ocean_state, diffusivity, bottom_drag, surface_forcing, land_sea, bottom_level):
    members, _, own, nx, ny = ocean_state.shape
    groups = slabs // 2
    rows = nx // slabs
    levels = diffusivity.shape[1]
    half_levels = levels // 2
    slab = lax.axis_index("slab")
    half = slab // groups
    group = slab % groups
    partner = [(i, (i + groups) % slabs) for i in range(slabs)]

    def swap(values):
        return lax.ppermute(values, "slab", partner)

    def cross(values):
        def moved(part):
            return [(i, (i // groups) * groups + ((i % groups) ^ part)) for i in range(slabs)]

        return [values[0]] + [lax.ppermute(values[part], "slab", moved(part)) for part in range(1, groups)]

    to_next = [(i, (i // groups) * groups + (i % groups + 1) % groups) for i in range(slabs)]
    to_prev = [(b, a) for a, b in to_next]

    scal = jnp.stack([group, half, slab * own]).astype(jnp.int32)

    view = ocean_state.reshape(members, 4, own, 2, groups, rows, ny)
    chunk_all = (members, 2, own, 2, rows, ny)
    chunk_level = (1, 2, 1, 2, rows, ny)
    v_send = call(
        functools.partial(split_kernel, groups, rows),
        "split",
        scal,
        (members, own),
        [(ocean_state, (1, 2, 1, nx, ny), lambda m, l, s: (m, 1, l, 0, 0))],
        [(chunk_all, chunk_level, lambda m, l, s: (m, 0, l, 0, 0, 0))] * groups,
        limit=60,
    )
    v_send, (diffusivity, bottom_drag, land_sea, bottom_level, ocean_late) = lax.optimization_barrier(
        (v_send, (diffusivity, bottom_drag, land_sea, bottom_level, ocean_state))
    )
    v_got = cross(v_send)

    f_got = swap(surface_forcing)
    give, own_other = call(
        functools.partial(give_kernel, half_levels),
        "give",
        scal,
        (members,),
        [
            (diffusivity, (1, levels, rows, ny), lambda m, s: (m, 0, 0, 0)),
            (bottom_drag, (1, rows, ny), lambda m, s: (m, 0, 0)),
            (land_sea, (1, rows, ny), lambda m, s: (m, s[1] * groups + s[0], 0)),
            (bottom_level, (1, rows, ny), lambda m, s: (m, s[1] * groups + s[0], 0)),
        ],
        [
            ((members, half_levels + 3, rows, ny), (1, half_levels + 3, rows, ny), lambda m, s: (m, 0, 0, 0)),
            ((members, 2, rows, ny), (1, 2, rows, ny), lambda m, s: (m, 0, 0, 0)),
        ],
    )
    give, land_sea, bottom_level, ocean_late = lax.optimization_barrier((give, land_sea, bottom_level, ocean_late))
    got = swap(give)

    f_tiles = jnp.where(half == 0, jnp.stack([surface_forcing, f_got], axis=2), 0.0)
    places = lax.axis_size("member")
    place = lax.axis_index("member")
    f_parts = [f_tiles] + [
        lax.ppermute(f_tiles, "member", [(i, (i + step) % places) for i in range(places)]) for step in range(1, places)
    ]
    forcing = jnp.concatenate([pick(f_parts, lax.rem(place - q + places, places)) for q in range(places)], axis=4)

    cell_n = jnp.where(land_sea == 1, bottom_level, 0)
    zonal_n = jnp.minimum(cell_n, jnp.roll(cell_n, -1, axis=1))
    merid_n = jnp.minimum(cell_n, jnp.concatenate([cell_n[:, :, 1:], jnp.zeros_like(cell_n[:, :, :1])], axis=2))

    def tiles(values):
        return lax.dynamic_index_in_dim(values.reshape(members, 2, groups, rows, ny), group, 2, keepdims=False)

    cell_t = tiles(cell_n)
    zonal_t = tiles(zonal_n)
    merid_t = tiles(merid_n)
    first_t = tiles(jnp.roll(zonal_n, 1, axis=1))[:, :, :1]

    t_send = call(
        functools.partial(advect_kernel, groups, rows),
        "advect",
        scal,
        (members, own),
        [
            (ocean_late, (1, 4, 1, nx, ny), lambda m, l, s: (m, 0, l, 0, 0)),
            (cell_n, (1, nx, ny), lambda m, l, s: (m, 0, 0)),
            (zonal_n, (1, nx, ny), lambda m, l, s: (m, 0, 0)),
            (merid_n, (1, nx, ny), lambda m, l, s: (m, 0, 0)),
        ],
        [(chunk_all, chunk_level, lambda m, l, s: (m, 0, l, 0, 0, 0))] * groups,
    )

    col_shape = (members, 2, half_levels, rows, ny)
    col_block = (1, 1, half_levels, rows, ny)
    mid_shape = (members, 2, 2, rows, ny)
    mid_block = (1, 1, 2, rows, ny)
    rate, inv_t, inv_v, mid, mid_other = call(
        functools.partial(factor_kernel, half_levels),
        "factor",
        scal,
        (members, 2),
        [
            (diffusivity, (1, levels, rows, ny), lambda m, t, s: (m, 0, 0, 0)),
            (got, (1, half_levels + 3, rows, ny), lambda m, t, s: (m, 0, 0, 0)),
            (bottom_drag, (1, rows, ny), lambda m, t, s: (m, 0, 0)),
            (own_other, (1, 2, rows, ny), lambda m, t, s: (m, 0, 0, 0)),
            (cell_t, (1, 1, rows, ny), lambda m, t, s: (m, t, 0, 0)),
        ],
        [
            (col_shape, col_block, lambda m, t, s: (m, t, 0, 0, 0)),
            (col_shape, col_block, lambda m, t, s: (m, t, 0, 0, 0)),
            (col_shape, col_block, lambda m, t, s: (m, t, 0, 0, 0)),
            (mid_shape, mid_block, lambda m, t, s: (m, t, 0, 0, 0)),
            (mid_shape, mid_block, lambda m, t, s: (m, t, 0, 0, 0)),
        ],
    )

    state_block = (1, 1, 2, half_levels, rows, ny)
    pair_block = (1, 1, 2, rows, ny)

    def at(m0):
        def mine(extra):
            return lambda m, t, s: (m, t) + (0,) * extra

        def shared(extra):
            return lambda m, t, s: (m + m0, t) + (0,) * extra

        return mine, shared

    def first(chunks, m0, count, inv, force_ids, masked):
        mine, shared = at(m0)
        return call(
            functools.partial(first_kernel, groups, own, force_ids, masked),
            "first",
            scal,
            (count, 2),
            [(c, (1, 2, own, 1, rows, ny), lambda m, t, s: (m + m0, 0, 0, t, 0, 0)) for c in chunks]
            + [
                (rate, col_block, shared(3)),
                (inv, col_block, shared(3)),
                (cell_t, (1, 1, rows, ny), shared(2)),
                (forcing, (1, 3, 1, rows, ny), lambda m, t, s: (0, 0, t, 0, 0)),
            ],
            [
                ((count, 2, 2, half_levels, rows, ny), state_block, mine(4)),
                ((count, 2, 2, rows, ny), pair_block, mine(3)),
            ],
            [pltpu.VMEM((2, half_levels, rows, ny), F32)],
        )

    def last(d, other, m0, count, inv, kind):
        mine, shared = at(m0)
        return call(
            functools.partial(last_kernel, groups, own, kind),
            "last",
            scal,
            (count, 2),
            [
                (d, state_block, mine(4)),
                (other, pair_block, mine(3)),
                (rate, col_block, shared(3)),
                (inv, col_block, shared(3)),
                (mid, pair_block, shared(3)),
                (mid_other, pair_block, shared(3)),
            ],
            [((count, 2, own, 2, rows, ny), (1, 2, own, 1, rows, ny), lambda m, t, s: (m, 0, 0, t, 0, 0))] * groups,
            [pltpu.VMEM((2, half_levels, rows, ny), F32)],
        )

    mine, shared = at(0)
    d_v, dm_v = first(v_got, 0, members, inv_v, (1, 2), False)
    t_send, dm_v = lax.optimization_barrier((t_send, dm_v))
    t_got = cross(t_send)
    dm_v_other = swap(dm_v)
    x_v, u_top, u_end, d2_v, dm2_v = call(
        middle_v_kernel,
        "middle_v",
        scal,
        (members, 2),
        [
            (d_v, state_block, mine(4)),
            (dm_v_other, pair_block, mine(3)),
            (rate, col_block, shared(3)),
            (inv_v, col_block, shared(3)),
            (mid, pair_block, shared(3)),
            (mid_other, pair_block, shared(3)),
            (cell_t, (1, 1, rows, ny), shared(2)),
            (forcing, (1, 3, 1, rows, ny), lambda m, t, s: (1, 0, t, 0, 0)),
        ],
        [
            ((members, 2, 2, half_levels, rows, ny), state_block, mine(4)),
            ((members, 2, half_levels, ny), (1, 1, half_levels, ny), mine(2)),
            ((members, 2, half_levels, ny), (1, 1, half_levels, ny), mine(2)),
            ((members, 2, 2, half_levels, rows, ny), state_block, mine(4)),
            ((members, 2, 2, rows, ny), pair_block, mine(3)),
        ],
    )
    dm2_v_other = swap(dm2_v)
    u_before = lax.ppermute(u_end, "slab", to_next)
    u_after = lax.ppermute(u_top, "slab", to_prev)
    d2_v, u_before, u_after = lax.optimization_barrier((d2_v, u_before, u_after))
    out_v = last(d2_v, dm2_v_other, 0, members, inv_v, 1)
    back_v = cross(out_v)

    back_t = []
    for m in range(1):
        mine, shared = at(m)
        d_t, dm_t = first(t_got, m, members, inv_t, (0, None), True)
        dm_t_other = swap(dm_t)
        x_t, t_top, t_end = call(
            middle_t_kernel,
            "middle_t",
            scal,
            (members, 2),
            [
                (d_t, state_block, mine(4)),
                (dm_t_other, pair_block, mine(3)),
                (rate, col_block, shared(3)),
                (inv_t, col_block, shared(3)),
                (mid, pair_block, shared(3)),
                (mid_other, pair_block, shared(3)),
            ],
            [
                ((members, 2, 2, half_levels, rows, ny), state_block, mine(4)),
                ((members, 2, 2, half_levels, ny), (1, 1, 2, half_levels, ny), mine(3)),
                ((members, 2, 2, half_levels, ny), (1, 1, 2, half_levels, ny), mine(3)),
            ],
        )
        t_before = lax.ppermute(t_end, "slab", to_next)
        t_after = lax.ppermute(t_top, "slab", to_prev)

        def from_before(extra, m0):
            return lambda i, t, s: (i + m0, t ^ jnp.where(s[0] == 0, 1, 0)) + (0,) * extra

        def from_after(extra, m0):
            return lambda i, t, s: (i + m0, t ^ jnp.where(s[0] == groups - 1, 1, 0)) + (0,) * extra

        x_t, back_v[1:-1] = lax.optimization_barrier((x_t, back_v[1:-1]))
        d2_t, dm2_t = call(
            second_t_kernel,
            "second_t",
            scal,
            (members, 2),
            [
                (x_t, state_block, mine(4)),
                (x_v, state_block, shared(4)),
                (t_before, (1, 1, 2, half_levels, ny), from_before(3, 0)),
                (t_after, (1, 1, 2, half_levels, ny), from_after(3, 0)),
                (u_before, (1, 1, half_levels, ny), from_before(2, m)),
                (u_after, (1, 1, half_levels, ny), from_after(2, m)),
                (rate, col_block, shared(3)),
                (inv_t, col_block, shared(3)),
                (cell_t, (1, 1, rows, ny), shared(2)),
                (zonal_t, (1, 1, rows, ny), shared(2)),
                (first_t, (1, 1, 1, ny), shared(2)),
                (merid_t, (1, 1, rows, ny), shared(2)),
                (forcing, (1, 3, 1, rows, ny), lambda i, t, s: (1, 0, t, 0, 0)),
            ],
            [
                ((members, 2, 2, half_levels, rows, ny), state_block, mine(4)),
                ((members, 2, 2, rows, ny), pair_block, mine(3)),
            ],
            [pltpu.VMEM((2, half_levels, rows, ny), F32)],
        )
        d2_t, back_v[-1] = lax.optimization_barrier((d2_t, back_v[-1]))
        back_t.append(cross(last(d2_t, swap(dm2_t), m, members, inv_t, 0)))

    whole = view.shape
    sems = [pltpu.SemaphoreType.DMA((groups,))]
    (result,) = call(
        functools.partial(place_kernel, groups, 0, 2, False),
        "place_v",
        scal,
        (),
        [(c, "VMEM", None) for c in back_v],
        [(whole, None, None)],
        sems,
    )
    for m in range(1):
        (result,) = call(
            functools.partial(place_kernel, groups, m, 0, True),
            "place_t",
            scal,
            (),
            [(c, "VMEM", None) for c in back_t[m]] + [(result, None, None)],
            [(whole, None, None)],
            sems,
            {groups + 1: 0},
        )
    return result.reshape(ocean_state.shape)


def solution(mesh):
    placed = (
        P("member", None, "slab", None, None),
        P("member", None, "slab", None),
        P("member", "slab", None),
        P(None, None, "slab", "member"),
        P("member", None, None),
        P("member", None, None),
    )
    return jax.shard_map(
        functools.partial(per_device, mesh.shape["slab"]),
        mesh=mesh,
        in_specs=placed,
        out_specs=P("member", None, "slab", None, None),
        check_vma=False,
    )
```

```python
import functools

import jax
import jax.numpy as jnp
from jax import lax
from jax.experimental import pallas as pl
from jax.experimental.pallas import tpu as pltpu
from jax.sharding import PartitionSpec as P

STEPS = 2
COURANT = 0.2
F32 = jnp.float32


def shift_next(block, after):
    rows = block.shape[0]
    row_ids = lax.broadcasted_iota(jnp.int32, block.shape, 0)
    return jnp.where(row_ids == rows - 1, after, pltpu.roll(block, rows - 1, 0))


def shift_prev(block, before):
    row_ids = lax.broadcasted_iota(jnp.int32, block.shape, 0)
    return jnp.where(row_ids == 0, before, pltpu.roll(block, 1, 0))


def lane_next(block):
    return pltpu.roll(block, block.shape[1] - 1, 1)


def lane_prev(block):
    return pltpu.roll(block, 1, 1)


def advect_tile(tracers, zonal, merid, counts, level):
    cell_n, zonal_n, zonal_first_n, merid_n = counts
    u, u_before, u_after = zonal
    face_u = jnp.where(level < zonal_n, 0.25 * (u + shift_next(u, u_after)), 0.0)
    first_u = jnp.where(level < zonal_first_n, 0.25 * (u_before + u[0:1]), 0.0)
    face_v = jnp.where(level < merid_n, 0.25 * (merid + lane_next(merid)), 0.0)
    out = []
    for c, c_before, c_after in tracers:
        flux_x = face_u * (c + shift_next(c, c_after))
        first_x = first_u * (c_before + c[0:1])
        flux_y = face_v * (c + lane_next(c))
        spread = (flux_x - shift_prev(flux_x, first_x)) + (flux_y - lane_prev(flux_y))
        out.append(jnp.where(level < cell_n, c - COURANT * spread, 0.0))
    return out


def advect_kernel(groups, rows, scal, state, cell_n, zonal_n, merid_n, *outs):
    nx = state.shape[3]
    level = scal[2] + pl.program_id(1)
    for part in range(groups):
        for tile in range(2):
            row0 = (tile * groups + (scal[0] ^ part)) * rows
            before = pl.multiple_of(lax.rem(row0 + nx - 8, nx), 8)
            after = pl.multiple_of(lax.rem(row0 + rows, nx), 8)
            here = pl.multiple_of(row0, 8)

            def whole(field):
                return (
                    state[0, field, 0, pl.ds(here, rows), :],
                    state[0, field, 0, pl.ds(before, 8), :][7:8],
                    state[0, field, 0, pl.ds(after, 8), :][0:1],
                )

            counts = (
                cell_n[0, pl.ds(here, rows), :],
                zonal_n[0, pl.ds(here, rows), :],
                zonal_n[0, pl.ds(before, 8), :][7:8],
                merid_n[0, pl.ds(here, rows), :],
            )
            merid = state[0, 3, 0, pl.ds(here, rows), :]
            moved = advect_tile([whole(0), whole(1)], whole(2), merid, counts, level)
            for field in range(2):
                outs[part][0, field, 0, tile] = moved[field]


def split_kernel(groups, scal, state, *refs):
    outs, sem = refs[:groups], refs[groups]
    copies = [
        pltpu.make_async_copy(state.at[:, pl.ds(2, 2), :, :, scal[0] ^ part], outs[part], sem.at[part])
        for part in range(groups)
    ]
    for copy in copies:
        copy.start()
    for copy in copies:
        copy.wait()


def give_kernel(half_levels, scal, own, drag, land, bottom, out, mid_other):
    half = scal[1]
    count = jnp.where(land[0] == 1, bottom[0], 0)
    shape = count.shape
    for e in range(half_levels):
        out[0, e] = own[0, (1 - half) * (half_levels - 1) + e]
    out[0, half_levels] = drag[0]

    def ends(which):
        top = which == 0
        prev = jnp.zeros(shape, F32)
        c_t = prev
        c_v = prev
        for e in range(half_levels):
            upper = jnp.where(top, e, 2 * half_levels - 2 - e)
            level = jnp.where(top, e, 2 * half_levels - 1 - e)
            r = jnp.where(upper + 1 < count, own[0, upper], 0.0)
            base = 1.0 + r
            c_v = r / (base + prev * (1.0 - c_v) + jnp.where(level == count - 1, drag[0], 0.0))
            c_t = r / (base + prev * (1.0 - c_t))
            prev = r
        return c_t, c_v

    mine = ends(half)
    others = ends(1 - half)
    for kind in range(2):
        out[0, half_levels + 1 + kind] = mine[kind]
        mid_other[0, kind] = others[kind]


def factor_kernel(half_levels, scal, own, got, own_drag, own_other, cell_n, rate, inv_t, inv_v, mid, mid_other):
    half = scal[1]
    tile = pl.program_id(1)
    top = half == 0
    start = half * (half_levels - 1)
    is_own = tile == half
    count = cell_n[0, 0]
    shape = count.shape
    drag = jnp.where(is_own, own_drag[0], got[0, half_levels])
    prev = jnp.zeros(shape, F32)
    c_t = prev
    c_v = prev
    for e in range(half_levels):
        spot = jnp.where(top, e, half_levels - 1 - e)
        deeper = jnp.where(top, e + 1, 2 * half_levels - 1 - e)
        level = jnp.where(top, e, 2 * half_levels - 1 - e)
        diff = jnp.where(is_own, own[0, start + spot], got[0, spot])
        r = jnp.where(deeper < count, diff, 0.0)
        base = 1.0 + r
        den_t = base + prev * (1.0 - c_t)
        den_v = base + prev * (1.0 - c_v) + jnp.where(level == count - 1, drag, 0.0)
        i_t = 1.0 / den_t
        i_v = 1.0 / den_v
        rate[0, 0, e] = r
        inv_t[0, 0, e] = i_t
        inv_v[0, 0, e] = i_v
        c_t = r * i_t
        c_v = r * i_v
        prev = r
    mid[0, 0, 0] = c_t
    mid[0, 0, 1] = c_v
    for kind in range(2):
        mid_other[0, 0, kind] = jnp.where(is_own, own_other[0, kind], got[0, half_levels + 1 + kind])


def sweep(rhs, rate, inv, store):
    half_levels = rate.shape[2]
    carry = [None, None]
    before = None
    for e in range(half_levels):
        inverse = inv[0, 0, e]
        for f in range(2):
            value = rhs(e, f)
            if e > 0:
                value = value + before * carry[f]
            carry[f] = value * inverse
            store(e, f, carry[f])
        before = rate[0, 0, e]
    return carry


def back(d_ref, other, rate, inv, mid, mid_other, kind, store):
    half_levels = rate.shape[2]
    last = half_levels - 1
    c_own = mid[0, 0, kind]
    c_oth = mid_other[0, 0, kind]
    scale = 1.0 / (1.0 - c_own * c_oth)
    value = [(d_ref[0, 0, f, last] + c_own * other[0, 0, f]) * scale for f in range(2)]
    for f in range(2):
        store(last, f, value[f])
    for e in range(last - 1, -1, -1):
        c = rate[0, 0, e] * inv[0, 0, e]
        for f in range(2):
            value[f] = d_ref[0, 0, f, e] + c * value[f]
            store(e, f, value[f])


def forced(forcing, count, force_ids, f):
    if force_ids[f] is None:
        return 0.0
    return jnp.where(count > 0, forcing[0, force_ids[f], 0], 0.0)


def slot_of(scal, part, lev, levels_own, half_levels):
    spot = (scal[0] ^ part) * levels_own + lev
    return jnp.where(scal[1] == 0, spot, half_levels - 1 - spot)


def first_kernel(groups, levels_own, force_ids, masked, scal, *refs):
    chunks = refs[:groups]
    rate, inv, cell_n, forcing, d_ref, mid_ref, buf = refs[groups:]
    half_levels = rate.shape[2]
    count = cell_n[0, 0]
    for part in range(groups):
        for lev in range(levels_own):
            slot = slot_of(scal, part, lev, levels_own, half_levels)
            level = scal[1] * half_levels + (scal[0] ^ part) * levels_own + lev
            for f in range(2):
                value = chunks[part][0, f, lev, 0]
                buf[f, slot] = value if masked else jnp.where(level < count, value, 0.0)

    def rhs(e, f):
        value = buf[f, e]
        return value + forced(forcing, count, force_ids, f) if e == 0 else value

    def store(e, f, value):
        d_ref[0, 0, f, e] = value

    carry = sweep(rhs, rate, inv, store)
    for f in range(2):
        mid_ref[0, 0, f] = carry[f]


def middle_v_kernel(scal, d_ref, other, rate, inv, mid, mid_other, cell_n, forcing, x_ref, top_ref, end_ref, d2_ref, mid2_ref):
    rows = x_ref.shape[4]

    def keep(e, f, value):
        x_ref[0, 0, f, e] = value
        if f == 0:
            top_ref[0, 0, pl.ds(e, 1), :] = value[0:1]
            end_ref[0, 0, pl.ds(e, 1), :] = value[rows - 1 : rows]

    back(d_ref, other, rate, inv, mid, mid_other, 1, keep)
    count = cell_n[0, 0]

    def rhs(e, f):
        value = x_ref[0, 0, f, e]
        return value + forced(forcing, count, (1, 2), f) if e == 0 else value

    def store(e, f, value):
        d2_ref[0, 0, f, e] = value

    carry = sweep(rhs, rate, inv, store)
    for f in range(2):
        mid2_ref[0, 0, f] = carry[f]


def middle_t_kernel(scal, d_ref, other, rate, inv, mid, mid_other, u_top, u_end, x_ref, top_ref, end_ref):
    rows = x_ref.shape[4]
    top_ref[0, 0, 2] = u_top[0, 0]
    end_ref[0, 0, 2] = u_end[0, 0]

    def keep(e, f, value):
        x_ref[0, 0, f, e] = value
        top_ref[0, 0, f, pl.ds(e, 1), :] = value[0:1]
        end_ref[0, 0, f, pl.ds(e, 1), :] = value[rows - 1 : rows]

    back(d_ref, other, rate, inv, mid, mid_other, 0, keep)


def second_t_kernel(scal, x_ref, v_ref, before, after, rate, inv, cell_n, zonal_n, first_n, merid_n, forcing, d_ref, mid_ref, buf):
    half_levels = rate.shape[2]
    top = scal[1] == 0
    count = cell_n[0, 0]
    counts = (count, zonal_n[0, 0], first_n[0, 0], merid_n[0, 0])
    for e in range(half_levels):
        level = jnp.where(top, e, 2 * half_levels - 1 - e)

        def edges(f):
            return before[0, 0, f, e : e + 1, :], after[0, 0, f, e : e + 1, :]

        tracers = [(x_ref[0, 0, f, e],) + edges(f) for f in range(2)]
        zonal = (v_ref[0, 0, 0, e],) + edges(2)
        moved = advect_tile(tracers, zonal, v_ref[0, 0, 1, e], counts, level)
        for f in range(2):
            buf[f, e] = moved[f]

    def rhs(e, f):
        value = buf[f, e]
        return value + forced(forcing, count, (0, None), f) if e == 0 else value

    def store(e, f, value):
        d_ref[0, 0, f, e] = value

    carry = sweep(rhs, rate, inv, store)
    for f in range(2):
        mid_ref[0, 0, f] = carry[f]


def last_kernel(groups, levels_own, kind, scal, d_ref, other, rate, inv, mid, mid_other, *refs):
    outs, buf = refs[:groups], refs[groups]
    half_levels = rate.shape[2]

    def keep(e, f, value):
        buf[f, e] = value

    back(d_ref, other, rate, inv, mid, mid_other, kind, keep)
    for part in range(groups):
        for lev in range(levels_own):
            slot = slot_of(scal, part, lev, levels_own, half_levels)
            for f in range(2):
                outs[part][0, f, lev, 0] = buf[f, slot]


def place_kernel(pieces, scal, *refs):
    chunks = refs[: len(pieces)]
    out, sem = refs[-2:]
    copies = []
    for index, (field, part) in enumerate(pieces):
        copies.append(
            pltpu.make_async_copy(
                chunks[index], out.at[:, pl.ds(field, 2), :, :, scal[0] ^ part], sem.at[index]
            )
        )
    for copy in copies:
        copy.start()
    for copy in copies:
        copy.wait()


def pick(values, which):
    out = values[0]
    for index in range(1, len(values)):
        out = jnp.where(which == index, values[index], out)
    return out


SPLIT_LIMIT = 40


def call(kernel, name, scal, grid, inputs, outputs, scratch=(), aliases=None, limit=40, weight=1 / 1024):
    def spec(block, index):
        if block is None:
            return pl.BlockSpec(memory_space=pl.ANY)
        if block == "VMEM":
            return pl.BlockSpec(memory_space=pltpu.VMEM)
        return pl.BlockSpec(block, index)

    bytes_moved = sum(a.size * 4 for a, b, _ in inputs if b is not None)
    for s, b, _ in outputs:
        size = 4
        for dim in s:
            size *= dim
        bytes_moved += size
    return pl.pallas_call(
        kernel,
        grid_spec=pltpu.PrefetchScalarGridSpec(
            num_scalar_prefetch=1,
            grid=grid,
            in_specs=[spec(b, i) for _, b, i in inputs],
            out_specs=[spec(b, i) for _, b, i in outputs],
            scratch_shapes=list(scratch),
        ),
        out_shape=[jax.ShapeDtypeStruct(s, F32) for s, _, _ in outputs],
        input_output_aliases=aliases or {},
        compiler_params=pltpu.CompilerParams(vmem_limit_bytes=limit * 1024 * 1024),
        cost_estimate=pl.CostEstimate(flops=0, bytes_accessed=int(bytes_moved * weight), transcendentals=0),
        name=name,
    )(scal, *[a for a, _, _ in inputs])


def per_device(slabs, ocean_state, diffusivity, bottom_drag, surface_forcing, land_sea, bottom_level):
    members, _, own, nx, ny = ocean_state.shape
    groups = slabs // 2
    rows = nx // slabs
    levels = diffusivity.shape[1]
    half_levels = levels // 2
    slab = lax.axis_index("slab")
    half = slab // groups
    group = slab % groups
    partner = [(i, (i + groups) % slabs) for i in range(slabs)]

    def swap(values):
        return lax.ppermute(values, "slab", partner)

    def cross(values, parts=range(1, groups)):
        def moved(part):
            return [(i, (i // groups) * groups + ((i % groups) ^ part)) for i in range(slabs)]

        return [values[0]] + [
            lax.ppermute(values[part], "slab", moved(part)) if part in parts else None for part in range(1, groups)
        ]

    to_next = [(i, (i // groups) * groups + (i % groups + 1) % groups) for i in range(slabs)]
    to_prev = [(b, a) for a, b in to_next]

    scal = jnp.stack([group, half, slab * own]).astype(jnp.int32)

    view = ocean_state.reshape(members, 4, own, 2, groups, rows, ny)
    chunk_all = (members, 2, own, 2, rows, ny)
    chunk_level = (1, 2, 1, 2, rows, ny)
    v_send = call(
        functools.partial(split_kernel, groups),
        "split",
        scal,
        (),
        [(view, None, None)],
        [(chunk_all, "VMEM", None)] * groups,
        [pltpu.SemaphoreType.DMA((groups,))],
        limit=SPLIT_LIMIT,
    )
    f_got = swap(surface_forcing)
    v_send, (diffusivity, bottom_drag, land_sea, bottom_level, ocean_late) = lax.optimization_barrier(
        (v_send, (diffusivity, bottom_drag, land_sea, bottom_level, ocean_state))
    )
    v_got = cross(v_send)

    give, own_other = call(
        functools.partial(give_kernel, half_levels),
        "give",
        scal,
        (members,),
        [
            (diffusivity, (1, levels, rows, ny), lambda m, s: (m, 0, 0, 0)),
            (bottom_drag, (1, rows, ny), lambda m, s: (m, 0, 0)),
            (land_sea, (1, rows, ny), lambda m, s: (m, s[1] * groups + s[0], 0)),
            (bottom_level, (1, rows, ny), lambda m, s: (m, s[1] * groups + s[0], 0)),
        ],
        [
            ((members, half_levels + 3, rows, ny), (1, half_levels + 3, rows, ny), lambda m, s: (m, 0, 0, 0)),
            ((members, 2, rows, ny), (1, 2, rows, ny), lambda m, s: (m, 0, 0, 0)),
        ],
    )
    give, land_sea, bottom_level, ocean_late = lax.optimization_barrier((give, land_sea, bottom_level, ocean_late))
    got = swap(give)

    f_tiles = jnp.where(half == 0, jnp.stack([surface_forcing, f_got], axis=2), 0.0)
    places = lax.axis_size("member")
    place = lax.axis_index("member")
    f_parts = [f_tiles] + [
        lax.ppermute(f_tiles, "member", [(i, (i + step) % places) for i in range(places)]) for step in range(1, places)
    ]
    forcing = jnp.concatenate([pick(f_parts, lax.rem(place - q + places, places)) for q in range(places)], axis=4)

    cell_n = jnp.where(land_sea == 1, bottom_level, 0)
    zonal_n = jnp.minimum(cell_n, jnp.roll(cell_n, -1, axis=1))
    merid_n = jnp.minimum(cell_n, jnp.concatenate([cell_n[:, :, 1:], jnp.zeros_like(cell_n[:, :, :1])], axis=2))

    def tiles(values):
        return lax.dynamic_index_in_dim(values.reshape(members, 2, groups, rows, ny), group, 2, keepdims=False)

    cell_t = tiles(cell_n)
    zonal_t = tiles(zonal_n)
    merid_t = tiles(merid_n)
    first_t = tiles(jnp.roll(zonal_n, 1, axis=1))[:, :, :1]

    t_send = call(
        functools.partial(advect_kernel, groups, rows),
        "advect",
        scal,
        (members, own),
        [
            (ocean_late, (1, 4, 1, nx, ny), lambda m, l, s: (m, 0, l, 0, 0)),
            (cell_n, (1, nx, ny), lambda m, l, s: (m, 0, 0)),
            (zonal_n, (1, nx, ny), lambda m, l, s: (m, 0, 0)),
            (merid_n, (1, nx, ny), lambda m, l, s: (m, 0, 0)),
        ],
        [(chunk_all, chunk_level, lambda m, l, s: (m, 0, l, 0, 0, 0))] * groups,
    )

    col_shape = (members, 2, half_levels, rows, ny)
    col_block = (1, 1, half_levels, rows, ny)
    mid_shape = (members, 2, 2, rows, ny)
    mid_block = (1, 1, 2, rows, ny)
    rate, inv_t, inv_v, mid, mid_other = call(
        functools.partial(factor_kernel, half_levels),
        "factor",
        scal,
        (members, 2),
        [
            (diffusivity, (1, levels, rows, ny), lambda m, t, s: (m, 0, 0, 0)),
            (got, (1, half_levels + 3, rows, ny), lambda m, t, s: (m, 0, 0, 0)),
            (bottom_drag, (1, rows, ny), lambda m, t, s: (m, 0, 0)),
            (own_other, (1, 2, rows, ny), lambda m, t, s: (m, 0, 0, 0)),
            (cell_t, (1, 1, rows, ny), lambda m, t, s: (m, t, 0, 0)),
        ],
        [
            (col_shape, col_block, lambda m, t, s: (m, t, 0, 0, 0)),
            (col_shape, col_block, lambda m, t, s: (m, t, 0, 0, 0)),
            (col_shape, col_block, lambda m, t, s: (m, t, 0, 0, 0)),
            (mid_shape, mid_block, lambda m, t, s: (m, t, 0, 0, 0)),
            (mid_shape, mid_block, lambda m, t, s: (m, t, 0, 0, 0)),
        ],
    )

    state_block = (1, 1, 2, half_levels, rows, ny)
    pair_block = (1, 1, 2, rows, ny)

    def at(m0):
        def mine(extra):
            return lambda m, t, s: (m, t) + (0,) * extra

        def shared(extra):
            return lambda m, t, s: (m + m0, t) + (0,) * extra

        return mine, shared

    def first(chunks, m0, count, inv, force_ids, masked):
        mine, shared = at(m0)
        return call(
            functools.partial(first_kernel, groups, own, force_ids, masked),
            "first",
            scal,
            (count, 2),
            [(c, (1, 2, own, 1, rows, ny), lambda m, t, s: (m + m0, 0, 0, t, 0, 0)) for c in chunks]
            + [
                (rate, col_block, shared(3)),
                (inv, col_block, shared(3)),
                (cell_t, (1, 1, rows, ny), shared(2)),
                (forcing, (1, 3, 1, rows, ny), lambda m, t, s: (0, 0, t, 0, 0)),
            ],
            [
                ((count, 2, 2, half_levels, rows, ny), state_block, mine(4)),
                ((count, 2, 2, rows, ny), pair_block, mine(3)),
            ],
            [pltpu.VMEM((2, half_levels, rows, ny), F32)],
        )

    def last(d, other, m0, count, inv, kind):
        mine, shared = at(m0)
        return call(
            functools.partial(last_kernel, groups, own, kind),
            "last",
            scal,
            (count, 2),
            [
                (d, state_block, mine(4)),
                (other, pair_block, mine(3)),
                (rate, col_block, shared(3)),
                (inv, col_block, shared(3)),
                (mid, pair_block, shared(3)),
                (mid_other, pair_block, shared(3)),
            ],
            [((count, 2, own, 2, rows, ny), (1, 2, own, 1, rows, ny), lambda m, t, s: (m, 0, 0, t, 0, 0))] * groups,
            [pltpu.VMEM((2, half_levels, rows, ny), F32)],
        )

    mine, shared = at(0)
    d_v, dm_v = first(v_got, 0, members, inv_v, (1, 2), False)
    t_send, dm_v = lax.optimization_barrier((list(t_send), dm_v))
    t_got = cross(t_send, range(1, groups - 1))
    dm_v_other = swap(dm_v)
    t_send[-1], dm_v_other = lax.optimization_barrier((t_send[-1], dm_v_other))
    t_got[-1] = cross(t_send, [groups - 1])[-1]
    d_t, dm_t = first(t_got, 0, members, inv_t, (0, None), True)
    x_v, u_top, u_end, d2_v, dm2_v = call(
        middle_v_kernel,
        "middle_v",
        scal,
        (members, 2),
        [
            (d_v, state_block, mine(4)),
            (dm_v_other, pair_block, mine(3)),
            (rate, col_block, shared(3)),
            (inv_v, col_block, shared(3)),
            (mid, pair_block, shared(3)),
            (mid_other, pair_block, shared(3)),
            (cell_t, (1, 1, rows, ny), shared(2)),
            (forcing, (1, 3, 1, rows, ny), lambda m, t, s: (1, 0, t, 0, 0)),
        ],
        [
            ((members, 2, 2, half_levels, rows, ny), state_block, mine(4)),
            ((members, 2, half_levels, ny), (1, 1, half_levels, ny), mine(2)),
            ((members, 2, half_levels, ny), (1, 1, half_levels, ny), mine(2)),
            ((members, 2, 2, half_levels, rows, ny), state_block, mine(4)),
            ((members, 2, 2, rows, ny), pair_block, mine(3)),
        ],
        weight=2,
    )
    dm2_v_other = swap(dm2_v)
    out_v = last(d2_v, dm2_v_other, 0, members, inv_v, 1)
    out_v, dm_t = lax.optimization_barrier((list(out_v), dm_t))
    back_v = cross(out_v, range(1, groups - 1))

    back_t = []
    for m in range(1):
        dm_t_other = swap(dm_t)
        mine, shared = at(m)
        x_t, t_top, t_end = call(
            middle_t_kernel,
            "middle_t",
            scal,
            (members, 2),
            [
                (d_t, state_block, mine(4)),
                (dm_t_other, pair_block, mine(3)),
                (rate, col_block, shared(3)),
                (inv_t, col_block, shared(3)),
                (mid, pair_block, shared(3)),
                (mid_other, pair_block, shared(3)),
                (u_top, (1, 1, half_levels, ny), mine(2)),
                (u_end, (1, 1, half_levels, ny), mine(2)),
            ],
            [
                ((members, 2, 2, half_levels, rows, ny), state_block, mine(4)),
                ((members, 2, 3, half_levels, ny), (1, 1, 3, half_levels, ny), mine(3)),
                ((members, 2, 3, half_levels, ny), (1, 1, 3, half_levels, ny), mine(3)),
            ],
        )
        t_before = lax.ppermute(t_end, "slab", to_next)
        t_after = lax.ppermute(t_top, "slab", to_prev)
        out_v[-1], t_before, t_after = lax.optimization_barrier((out_v[-1], t_before, t_after))
        back_v[-1] = cross(out_v, [groups - 1])[-1]

        def from_before(extra, m0):
            return lambda i, t, s: (i + m0, t ^ jnp.where(s[0] == 0, 1, 0)) + (0,) * extra

        def from_after(extra, m0):
            return lambda i, t, s: (i + m0, t ^ jnp.where(s[0] == groups - 1, 1, 0)) + (0,) * extra

        x_t, back_v[1:-1] = lax.optimization_barrier((x_t, back_v[1:-1]))
        d2_t, dm2_t = call(
            second_t_kernel,
            "second_t",
            scal,
            (members, 2),
            [
                (x_t, state_block, mine(4)),
                (x_v, state_block, shared(4)),
                (t_before, (1, 1, 3, half_levels, ny), from_before(3, 0)),
                (t_after, (1, 1, 3, half_levels, ny), from_after(3, 0)),
                (rate, col_block, shared(3)),
                (inv_t, col_block, shared(3)),
                (cell_t, (1, 1, rows, ny), shared(2)),
                (zonal_t, (1, 1, rows, ny), shared(2)),
                (first_t, (1, 1, 1, ny), shared(2)),
                (merid_t, (1, 1, rows, ny), shared(2)),
                (forcing, (1, 3, 1, rows, ny), lambda i, t, s: (1, 0, t, 0, 0)),
            ],
            [
                ((members, 2, 2, half_levels, rows, ny), state_block, mine(4)),
                ((members, 2, 2, rows, ny), pair_block, mine(3)),
            ],
            [pltpu.VMEM((2, half_levels, rows, ny), F32)],
        )
        d2_t, back_v[-1] = lax.optimization_barrier((d2_t, back_v[-1]))
        back_t.append(cross(last(d2_t, swap(dm2_t), m, members, inv_t, 0)))

    whole = view.shape
    chunks = {(2, part): back_v[part] for part in range(groups)}
    chunks.update({(0, part): back_t[0][part] for part in range(groups)})
    pieces = list(chunks)
    result = None
    for some in (pieces[: groups + 1], pieces[groups + 1 : -1], pieces[-1:]):
        held = [] if result is None else [(result, None, None)]
        (result,) = call(
            functools.partial(place_kernel, some),
            "place",
            scal,
            (),
            [(chunks[piece], "VMEM", None) for piece in some] + held,
            [(whole, None, None)],
            [pltpu.SemaphoreType.DMA((len(some),))],
            {len(some) + 1: 0} if held else None,
        )
    return result.reshape(ocean_state.shape)


def solution(mesh):
    placed = (
        P("member", None, "slab", None, None),
        P("member", None, "slab", None),
        P("member", "slab", None),
        P(None, None, "slab", "member"),
        P("member", None, None),
        P("member", None, None),
    )
    return jax.shard_map(
        functools.partial(per_device, mesh.shape["slab"]),
        mesh=mesh,
        in_specs=placed,
        out_specs=P("member", None, "slab", None, None),
        check_vma=False,
    )
```

```python
import functools

import jax
import jax.numpy as jnp
from jax import lax
from jax.experimental import pallas as pl
from jax.experimental.pallas import tpu as pltpu
from jax.sharding import PartitionSpec as P

STEPS = 2
COURANT = 0.2
F32 = jnp.float32


def shift_next(block, after):
    rows = block.shape[0]
    row_ids = lax.broadcasted_iota(jnp.int32, block.shape, 0)
    return jnp.where(row_ids == rows - 1, after, pltpu.roll(block, rows - 1, 0))


def shift_prev(block, before):
    row_ids = lax.broadcasted_iota(jnp.int32, block.shape, 0)
    return jnp.where(row_ids == 0, before, pltpu.roll(block, 1, 0))


def lane_next(block):
    return pltpu.roll(block, block.shape[1] - 1, 1)


def lane_prev(block):
    return pltpu.roll(block, 1, 1)


def advect_tile(tracers, zonal, merid, counts, level):
    cell_n, zonal_n, zonal_first_n, merid_n = counts
    u, u_before, u_after = zonal
    face_u = jnp.where(level < zonal_n, 0.25 * (u + shift_next(u, u_after)), 0.0)
    first_u = jnp.where(level < zonal_first_n, 0.25 * (u_before + u[0:1]), 0.0)
    face_v = jnp.where(level < merid_n, 0.25 * (merid + lane_next(merid)), 0.0)
    out = []
    for c, c_before, c_after in tracers:
        flux_x = face_u * (c + shift_next(c, c_after))
        first_x = first_u * (c_before + c[0:1])
        flux_y = face_v * (c + lane_next(c))
        spread = (flux_x - shift_prev(flux_x, first_x)) + (flux_y - lane_prev(flux_y))
        out.append(jnp.where(level < cell_n, c - COURANT * spread, 0.0))
    return out


def advect_kernel(groups, rows, scal, state, cell_n, zonal_n, merid_n, *outs):
    nx = state.shape[3]
    level = scal[2] + pl.program_id(1)
    for part in range(groups):
        for tile in range(2):
            row0 = (tile * groups + (scal[0] ^ part)) * rows
            before = pl.multiple_of(lax.rem(row0 + nx - 8, nx), 8)
            after = pl.multiple_of(lax.rem(row0 + rows, nx), 8)
            here = pl.multiple_of(row0, 8)

            def whole(field):
                return (
                    state[0, field, 0, pl.ds(here, rows), :],
                    state[0, field, 0, pl.ds(before, 8), :][7:8],
                    state[0, field, 0, pl.ds(after, 8), :][0:1],
                )

            counts = (
                cell_n[0, pl.ds(here, rows), :],
                zonal_n[0, pl.ds(here, rows), :],
                zonal_n[0, pl.ds(before, 8), :][7:8],
                merid_n[0, pl.ds(here, rows), :],
            )
            merid = state[0, 3, 0, pl.ds(here, rows), :]
            moved = advect_tile([whole(0), whole(1)], whole(2), merid, counts, level)
            for field in range(2):
                outs[part][0, field, 0, tile] = moved[field]


def split_kernel(groups, scal, state, *refs):
    outs, sem = refs[:groups], refs[groups]
    copies = [
        pltpu.make_async_copy(state.at[:, pl.ds(2, 2), :, :, scal[0] ^ part], outs[part], sem.at[part])
        for part in range(groups)
    ]
    for copy in copies:
        copy.start()
    for copy in copies:
        copy.wait()


def give_kernel(half_levels, scal, own, drag, land, bottom, out, mid_other):
    half = scal[1]
    count = jnp.where(land[0] == 1, bottom[0], 0)
    shape = count.shape
    for e in range(half_levels):
        out[0, e] = own[0, (1 - half) * (half_levels - 1) + e]
    out[0, half_levels] = drag[0]

    def ends(which):
        top = which == 0
        prev = jnp.zeros(shape, F32)
        c_t = prev
        c_v = prev
        for e in range(half_levels):
            upper = jnp.where(top, e, 2 * half_levels - 2 - e)
            level = jnp.where(top, e, 2 * half_levels - 1 - e)
            r = jnp.where(upper + 1 < count, own[0, upper], 0.0)
            base = 1.0 + r
            c_v = r / (base + prev * (1.0 - c_v) + jnp.where(level == count - 1, drag[0], 0.0))
            c_t = r / (base + prev * (1.0 - c_t))
            prev = r
        return c_t, c_v

    mine = ends(half)
    others = ends(1 - half)
    for kind in range(2):
        out[0, half_levels + 1 + kind] = mine[kind]
        mid_other[0, kind] = others[kind]


def factor_kernel(half_levels, scal, own, got, own_drag, own_other, cell_n, rate, inv_t, inv_v, mid, mid_other):
    half = scal[1]
    tile = pl.program_id(1)
    top = half == 0
    start = half * (half_levels - 1)
    is_own = tile == half
    count = cell_n[0, 0]
    shape = count.shape
    drag = jnp.where(is_own, own_drag[0], got[0, half_levels])
    prev = jnp.zeros(shape, F32)
    c_t = prev
    c_v = prev
    for e in range(half_levels):
        spot = jnp.where(top, e, half_levels - 1 - e)
        deeper = jnp.where(top, e + 1, 2 * half_levels - 1 - e)
        level = jnp.where(top, e, 2 * half_levels - 1 - e)
        diff = jnp.where(is_own, own[0, start + spot], got[0, spot])
        r = jnp.where(deeper < count, diff, 0.0)
        base = 1.0 + r
        den_t = base + prev * (1.0 - c_t)
        den_v = base + prev * (1.0 - c_v) + jnp.where(level == count - 1, drag, 0.0)
        i_t = 1.0 / den_t
        i_v = 1.0 / den_v
        rate[0, 0, e] = r
        inv_t[0, 0, e] = i_t
        inv_v[0, 0, e] = i_v
        c_t = r * i_t
        c_v = r * i_v
        prev = r
    mid[0, 0, 0] = c_t
    mid[0, 0, 1] = c_v
    for kind in range(2):
        mid_other[0, 0, kind] = jnp.where(is_own, own_other[0, kind], got[0, half_levels + 1 + kind])


def sweep(rhs, rate, inv, store):
    half_levels = rate.shape[2]
    carry = [None, None]
    before = None
    for e in range(half_levels):
        inverse = inv[0, 0, e]
        for f in range(2):
            value = rhs(e, f)
            if e > 0:
                value = value + before * carry[f]
            carry[f] = value * inverse
            store(e, f, carry[f])
        before = rate[0, 0, e]
    return carry


def back(d_ref, other, rate, inv, mid, mid_other, kind, store):
    half_levels = rate.shape[2]
    last = half_levels - 1
    c_own = mid[0, 0, kind]
    c_oth = mid_other[0, 0, kind]
    scale = 1.0 / (1.0 - c_own * c_oth)
    value = [(d_ref[0, 0, f, last] + c_own * other[0, 0, f]) * scale for f in range(2)]
    for f in range(2):
        store(last, f, value[f])
    for e in range(last - 1, -1, -1):
        c = rate[0, 0, e] * inv[0, 0, e]
        for f in range(2):
            value[f] = d_ref[0, 0, f, e] + c * value[f]
            store(e, f, value[f])


def forced(forcing, count, force_ids, f):
    if force_ids[f] is None:
        return 0.0
    return jnp.where(count > 0, forcing[0, force_ids[f], 0], 0.0)


def slot_of(scal, part, lev, levels_own, half_levels):
    spot = (scal[0] ^ part) * levels_own + lev
    return jnp.where(scal[1] == 0, spot, half_levels - 1 - spot)


def first_kernel(parts, levels_own, force_ids, masked, scal, *refs):
    groups = len(parts)
    chunks = refs[:groups]
    rate, inv, cell_n, forcing, d_ref, mid_ref, buf = refs[groups:]
    half_levels = rate.shape[2]
    count = cell_n[0, 0]
    for chunk, part in zip(chunks, parts):
        for lev in range(levels_own):
            slot = slot_of(scal, part, lev, levels_own, half_levels)
            level = scal[1] * half_levels + (scal[0] ^ part) * levels_own + lev
            for f in range(2):
                value = chunk[0, f, lev, 0]
                buf[f, slot] = value if masked else jnp.where(level < count, value, 0.0)

    def rhs(e, f):
        value = buf[f, e]
        return value + forced(forcing, count, force_ids, f) if e == 0 else value

    def store(e, f, value):
        d_ref[0, 0, f, e] = value

    carry = sweep(rhs, rate, inv, store)
    for f in range(2):
        mid_ref[0, 0, f] = carry[f]


def middle_v_kernel(scal, d_ref, other, rate, inv, mid, mid_other, cell_n, forcing, x_ref, top_ref, end_ref, d2_ref, mid2_ref):
    rows = x_ref.shape[4]

    def keep(e, f, value):
        x_ref[0, 0, f, e] = value
        if f == 0:
            top_ref[0, 0, pl.ds(e, 1), :] = value[0:1]
            end_ref[0, 0, pl.ds(e, 1), :] = value[rows - 1 : rows]

    back(d_ref, other, rate, inv, mid, mid_other, 1, keep)
    count = cell_n[0, 0]

    def rhs(e, f):
        value = x_ref[0, 0, f, e]
        return value + forced(forcing, count, (1, 2), f) if e == 0 else value

    def store(e, f, value):
        d2_ref[0, 0, f, e] = value

    carry = sweep(rhs, rate, inv, store)
    for f in range(2):
        mid2_ref[0, 0, f] = carry[f]


def middle_t_kernel(scal, d_ref, other, rate, inv, mid, mid_other, u_top, u_end, x_ref, top_ref, end_ref):
    rows = x_ref.shape[4]
    top_ref[0, 0, 2] = u_top[0, 0]
    end_ref[0, 0, 2] = u_end[0, 0]

    def keep(e, f, value):
        x_ref[0, 0, f, e] = value
        top_ref[0, 0, f, pl.ds(e, 1), :] = value[0:1]
        end_ref[0, 0, f, pl.ds(e, 1), :] = value[rows - 1 : rows]

    back(d_ref, other, rate, inv, mid, mid_other, 0, keep)


def second_t_kernel(scal, x_ref, v_ref, before, after, rate, inv, cell_n, zonal_n, first_n, merid_n, forcing, d_ref, mid_ref, buf):
    half_levels = rate.shape[2]
    top = scal[1] == 0
    count = cell_n[0, 0]
    counts = (count, zonal_n[0, 0], first_n[0, 0], merid_n[0, 0])
    for e in range(half_levels):
        level = jnp.where(top, e, 2 * half_levels - 1 - e)

        def edges(f):
            return before[0, 0, f, e : e + 1, :], after[0, 0, f, e : e + 1, :]

        tracers = [(x_ref[0, 0, f, e],) + edges(f) for f in range(2)]
        zonal = (v_ref[0, 0, 0, e],) + edges(2)
        moved = advect_tile(tracers, zonal, v_ref[0, 0, 1, e], counts, level)
        for f in range(2):
            buf[f, e] = moved[f]

    def rhs(e, f):
        value = buf[f, e]
        return value + forced(forcing, count, (0, None), f) if e == 0 else value

    def store(e, f, value):
        d_ref[0, 0, f, e] = value

    carry = sweep(rhs, rate, inv, store)
    for f in range(2):
        mid_ref[0, 0, f] = carry[f]


def last_kernel(groups, levels_own, kind, scal, d_ref, other, rate, inv, mid, mid_other, *refs):
    outs, buf = refs[:groups], refs[groups]
    half_levels = rate.shape[2]

    def keep(e, f, value):
        buf[f, e] = value

    back(d_ref, other, rate, inv, mid, mid_other, kind, keep)
    for part in range(groups):
        for lev in range(levels_own):
            slot = slot_of(scal, part, lev, levels_own, half_levels)
            for f in range(2):
                outs[part][0, f, lev, 0] = buf[f, slot]


def place_kernel(pieces, scal, *refs):
    chunks = refs[: len(pieces)]
    out, sem = refs[-2:]
    copies = []
    for index, (field, part) in enumerate(pieces):
        copies.append(
            pltpu.make_async_copy(
                chunks[index], out.at[:, pl.ds(field, 2), :, :, scal[0] ^ part], sem.at[index]
            )
        )
    for copy in copies:
        copy.start()
    for copy in copies:
        copy.wait()


def pick(values, which):
    out = values[0]
    for index in range(1, len(values)):
        out = jnp.where(which == index, values[index], out)
    return out


SPLIT_LIMIT = 40


def call(kernel, name, scal, grid, inputs, outputs, scratch=(), aliases=None, limit=40, weight=1 / 1024):
    def spec(block, index):
        if block is None:
            return pl.BlockSpec(memory_space=pl.ANY)
        if block == "VMEM":
            return pl.BlockSpec(memory_space=pltpu.VMEM)
        return pl.BlockSpec(block, index)

    bytes_moved = sum(a.size * 4 for a, b, _ in inputs if b is not None)
    for s, b, _ in outputs:
        size = 4
        for dim in s:
            size *= dim
        bytes_moved += size
    return pl.pallas_call(
        kernel,
        grid_spec=pltpu.PrefetchScalarGridSpec(
            num_scalar_prefetch=1,
            grid=grid,
            in_specs=[spec(b, i) for _, b, i in inputs],
            out_specs=[spec(b, i) for _, b, i in outputs],
            scratch_shapes=list(scratch),
        ),
        out_shape=[jax.ShapeDtypeStruct(s, F32) for s, _, _ in outputs],
        input_output_aliases=aliases or {},
        compiler_params=pltpu.CompilerParams(vmem_limit_bytes=limit * 1024 * 1024),
        cost_estimate=pl.CostEstimate(flops=0, bytes_accessed=int(bytes_moved * weight), transcendentals=0),
        name=name,
    )(scal, *[a for a, _, _ in inputs])


def per_device(slabs, ocean_state, diffusivity, bottom_drag, surface_forcing, land_sea, bottom_level):
    members, _, own, nx, ny = ocean_state.shape
    groups = slabs // 2
    rows = nx // slabs
    levels = diffusivity.shape[1]
    half_levels = levels // 2
    slab = lax.axis_index("slab")
    half = slab // groups
    group = slab % groups
    partner = [(i, (i + groups) % slabs) for i in range(slabs)]

    def swap(values):
        return lax.ppermute(values, "slab", partner)

    def cross(values, parts=range(1, groups)):
        def moved(part):
            return [(i, (i // groups) * groups + ((i % groups) ^ part)) for i in range(slabs)]

        return [values[0]] + [
            lax.ppermute(values[part], "slab", moved(part)) if part in parts else None for part in range(1, groups)
        ]

    to_next = [(i, (i // groups) * groups + (i % groups + 1) % groups) for i in range(slabs)]
    to_prev = [(b, a) for a, b in to_next]

    scal = jnp.stack([group, half, slab * own]).astype(jnp.int32)

    view = ocean_state.reshape(members, 4, own, 2, groups, rows, ny)
    chunk_all = (members, 2, own, 2, rows, ny)
    chunk_level = (1, 2, 1, 2, rows, ny)
    v_send = call(
        functools.partial(split_kernel, groups),
        "split",
        scal,
        (),
        [(pltpu.with_memory_space_constraint(view, pltpu.HBM), None, None)],
        [(chunk_all, "VMEM", None)] * groups,
        [pltpu.SemaphoreType.DMA((groups,))],
        limit=SPLIT_LIMIT,
    )
    f_got = swap(surface_forcing)
    v_send, (diffusivity, bottom_drag, land_sea, bottom_level, ocean_late) = lax.optimization_barrier(
        (v_send, (diffusivity, bottom_drag, land_sea, bottom_level, ocean_state))
    )
    v_got = cross(v_send)

    give, own_other = call(
        functools.partial(give_kernel, half_levels),
        "give",
        scal,
        (members,),
        [
            (diffusivity, (1, levels, rows, ny), lambda m, s: (m, 0, 0, 0)),
            (bottom_drag, (1, rows, ny), lambda m, s: (m, 0, 0)),
            (land_sea, (1, rows, ny), lambda m, s: (m, s[1] * groups + s[0], 0)),
            (bottom_level, (1, rows, ny), lambda m, s: (m, s[1] * groups + s[0], 0)),
        ],
        [
            ((members, half_levels + 3, rows, ny), (1, half_levels + 3, rows, ny), lambda m, s: (m, 0, 0, 0)),
            ((members, 2, rows, ny), (1, 2, rows, ny), lambda m, s: (m, 0, 0, 0)),
        ],
    )
    give, land_sea, bottom_level, ocean_late = lax.optimization_barrier((give, land_sea, bottom_level, ocean_late))
    got = swap(give)

    f_tiles = jnp.where(half == 0, jnp.stack([surface_forcing, f_got], axis=2), 0.0)
    places = lax.axis_size("member")
    place = lax.axis_index("member")
    f_parts = [f_tiles] + [
        lax.ppermute(f_tiles, "member", [(i, (i + step) % places) for i in range(places)]) for step in range(1, places)
    ]
    forcing = jnp.concatenate([pick(f_parts, lax.rem(place - q + places, places)) for q in range(places)], axis=4)

    cell_n = jnp.where(land_sea == 1, bottom_level, 0)
    zonal_n = jnp.minimum(cell_n, jnp.roll(cell_n, -1, axis=1))
    merid_n = jnp.minimum(cell_n, jnp.concatenate([cell_n[:, :, 1:], jnp.zeros_like(cell_n[:, :, :1])], axis=2))

    def tiles(values):
        return lax.dynamic_index_in_dim(values.reshape(members, 2, groups, rows, ny), group, 2, keepdims=False)

    cell_t = tiles(cell_n)
    zonal_t = tiles(zonal_n)
    merid_t = tiles(merid_n)
    first_t = tiles(jnp.roll(zonal_n, 1, axis=1))[:, :, :1]

    t_send = call(
        functools.partial(advect_kernel, groups, rows),
        "advect",
        scal,
        (members, own),
        [
            (ocean_late, (1, 4, 1, nx, ny), lambda m, l, s: (m, 0, l, 0, 0)),
            (cell_n, (1, nx, ny), lambda m, l, s: (m, 0, 0)),
            (zonal_n, (1, nx, ny), lambda m, l, s: (m, 0, 0)),
            (merid_n, (1, nx, ny), lambda m, l, s: (m, 0, 0)),
        ],
        [(chunk_all, chunk_level, lambda m, l, s: (m, 0, l, 0, 0, 0))] * groups,
    )

    t_send = list(t_send)
    t_send[:-1], got, forcing = lax.optimization_barrier((t_send[:-1], got, forcing))
    t_got = cross(t_send, range(1, groups - 1))

    col_shape = (members, 2, half_levels, rows, ny)
    col_block = (1, 1, half_levels, rows, ny)
    mid_shape = (members, 2, 2, rows, ny)
    mid_block = (1, 1, 2, rows, ny)
    rate, inv_t, inv_v, mid, mid_other = call(
        functools.partial(factor_kernel, half_levels),
        "factor",
        scal,
        (members, 2),
        [
            (diffusivity, (1, levels, rows, ny), lambda m, t, s: (m, 0, 0, 0)),
            (got, (1, half_levels + 3, rows, ny), lambda m, t, s: (m, 0, 0, 0)),
            (pltpu.with_memory_space_constraint(bottom_drag, pltpu.HBM), (1, rows, ny), lambda m, t, s: (m, 0, 0)),
            (pltpu.with_memory_space_constraint(own_other, pltpu.HBM), (1, 2, rows, ny), lambda m, t, s: (m, 0, 0, 0)),
            (cell_t, (1, 1, rows, ny), lambda m, t, s: (m, t, 0, 0)),
        ],
        [
            (col_shape, col_block, lambda m, t, s: (m, t, 0, 0, 0)),
            (col_shape, col_block, lambda m, t, s: (m, t, 0, 0, 0)),
            (col_shape, col_block, lambda m, t, s: (m, t, 0, 0, 0)),
            (mid_shape, mid_block, lambda m, t, s: (m, t, 0, 0, 0)),
            (mid_shape, mid_block, lambda m, t, s: (m, t, 0, 0, 0)),
        ],
    )

    state_block = (1, 1, 2, half_levels, rows, ny)
    pair_block = (1, 1, 2, rows, ny)

    def at(m0):
        def mine(extra):
            return lambda m, t, s: (m, t) + (0,) * extra

        def shared(extra):
            return lambda m, t, s: (m + m0, t) + (0,) * extra

        return mine, shared

    def first(chunks, m0, count, inv, force_ids, masked, parts):
        mine, shared = at(m0)
        return call(
            functools.partial(first_kernel, tuple(parts), own, force_ids, masked),
            "first",
            scal,
            (count, 2),
            [(c, (1, 2, own, 1, rows, ny), lambda m, t, s: (m + m0, 0, 0, t, 0, 0)) for c in (chunks[p] for p in parts)]
            + [
                (rate, col_block, shared(3)),
                (inv, col_block, shared(3)),
                (cell_t, (1, 1, rows, ny), shared(2)),
                (forcing, (1, 3, 1, rows, ny), lambda m, t, s: (0, 0, t, 0, 0)),
            ],
            [
                ((count, 2, 2, half_levels, rows, ny), state_block, mine(4)),
                ((count, 2, 2, rows, ny), pair_block, mine(3)),
            ],
            [pltpu.VMEM((2, half_levels, rows, ny), F32)],
            weight=4,
        )

    def last(d, other, m0, count, inv, kind):
        mine, shared = at(m0)
        return call(
            functools.partial(last_kernel, groups, own, kind),
            "last",
            scal,
            (count, 2),
            [
                (d, state_block, mine(4)),
                (other, pair_block, mine(3)),
                (rate, col_block, shared(3)),
                (inv, col_block, shared(3)),
                (mid, pair_block, shared(3)),
                (mid_other, pair_block, shared(3)),
            ],
            [((count, 2, own, 2, rows, ny), (1, 2, own, 1, rows, ny), lambda m, t, s: (m, 0, 0, t, 0, 0))] * groups,
            [pltpu.VMEM((2, half_levels, rows, ny), F32)],
        )

    mine, shared = at(0)
    d_v, dm_v = first(v_got, 0, members, inv_v, (1, 2), False, [0, groups - 1] + list(range(1, groups - 1)))
    dm_v_other = swap(dm_v)
    t_send[-1], dm_v = lax.optimization_barrier((t_send[-1], dm_v))
    dm_v_other, t_got[1:-1] = lax.optimization_barrier((dm_v_other, t_got[1:-1]))
    t_got[-1] = cross(t_send, [groups - 1])[-1]
    d_t, dm_t = first(t_got, 0, members, inv_t, (0, None), True, range(groups))
    x_v, u_top, u_end, d2_v, dm2_v = call(
        middle_v_kernel,
        "middle_v",
        scal,
        (members, 2),
        [
            (d_v, state_block, mine(4)),
            (dm_v_other, pair_block, mine(3)),
            (rate, col_block, shared(3)),
            (inv_v, col_block, shared(3)),
            (mid, pair_block, shared(3)),
            (mid_other, pair_block, shared(3)),
            (cell_t, (1, 1, rows, ny), shared(2)),
            (forcing, (1, 3, 1, rows, ny), lambda m, t, s: (1, 0, t, 0, 0)),
        ],
        [
            ((members, 2, 2, half_levels, rows, ny), state_block, mine(4)),
            ((members, 2, half_levels, ny), (1, 1, half_levels, ny), mine(2)),
            ((members, 2, half_levels, ny), (1, 1, half_levels, ny), mine(2)),
            ((members, 2, 2, half_levels, rows, ny), state_block, mine(4)),
            ((members, 2, 2, rows, ny), pair_block, mine(3)),
        ],
        weight=2,
    )
    dm2_v_other = swap(dm2_v)
    out_v = last(d2_v, dm2_v_other, 0, members, inv_v, 1)
    out_v, dm_t = lax.optimization_barrier((list(out_v), dm_t))
    back_v = cross(out_v, range(1, groups - 1))

    back_t = []
    for m in range(1):
        dm_t_other = swap(dm_t)
        mine, shared = at(m)
        x_t, t_top, t_end = call(
            middle_t_kernel,
            "middle_t",
            scal,
            (members, 2),
            [
                (d_t, state_block, mine(4)),
                (dm_t_other, pair_block, mine(3)),
                (rate, col_block, shared(3)),
                (inv_t, col_block, shared(3)),
                (mid, pair_block, shared(3)),
                (mid_other, pair_block, shared(3)),
                (u_top, (1, 1, half_levels, ny), mine(2)),
                (u_end, (1, 1, half_levels, ny), mine(2)),
            ],
            [
                ((members, 2, 2, half_levels, rows, ny), state_block, mine(4)),
                ((members, 2, 3, half_levels, ny), (1, 1, 3, half_levels, ny), mine(3)),
                ((members, 2, 3, half_levels, ny), (1, 1, 3, half_levels, ny), mine(3)),
            ],
        )
        t_before = lax.ppermute(t_end, "slab", to_next)
        t_after = lax.ppermute(t_top, "slab", to_prev)
        out_v[-1], t_before, t_after = lax.optimization_barrier((out_v[-1], t_before, t_after))
        back_v[-1] = cross(out_v, [groups - 1])[-1]

        def from_before(extra, m0):
            return lambda i, t, s: (i + m0, t ^ jnp.where(s[0] == 0, 1, 0)) + (0,) * extra

        def from_after(extra, m0):
            return lambda i, t, s: (i + m0, t ^ jnp.where(s[0] == groups - 1, 1, 0)) + (0,) * extra

        x_t, back_v[1:-1] = lax.optimization_barrier((x_t, back_v[1:-1]))
        d2_t, dm2_t = call(
            second_t_kernel,
            "second_t",
            scal,
            (members, 2),
            [
                (x_t, state_block, mine(4)),
                (x_v, state_block, shared(4)),
                (t_before, (1, 1, 3, half_levels, ny), from_before(3, 0)),
                (t_after, (1, 1, 3, half_levels, ny), from_after(3, 0)),
                (rate, col_block, shared(3)),
                (inv_t, col_block, shared(3)),
                (cell_t, (1, 1, rows, ny), shared(2)),
                (zonal_t, (1, 1, rows, ny), shared(2)),
                (first_t, (1, 1, 1, ny), shared(2)),
                (merid_t, (1, 1, rows, ny), shared(2)),
                (forcing, (1, 3, 1, rows, ny), lambda i, t, s: (1, 0, t, 0, 0)),
            ],
            [
                ((members, 2, 2, half_levels, rows, ny), state_block, mine(4)),
                ((members, 2, 2, rows, ny), pair_block, mine(3)),
            ],
            [pltpu.VMEM((2, half_levels, rows, ny), F32)],
        )
        d2_t, back_v[-1] = lax.optimization_barrier((d2_t, back_v[-1]))
        back_t.append(cross(last(d2_t, swap(dm2_t), m, members, inv_t, 0)))

    whole = view.shape
    chunks = {(2, part): back_v[part] for part in range(groups)}
    chunks.update({(0, part): back_t[0][part] for part in range(groups)})
    pieces = list(chunks)
    result = None
    for some in (pieces[: groups + 1], pieces[groups + 1 : -1], pieces[-1:]):
        held = [] if result is None else [(result, None, None)]
        (result,) = call(
            functools.partial(place_kernel, some),
            "place",
            scal,
            (),
            [(chunks[piece], "VMEM", None) for piece in some] + held,
            [(whole, None, None)],
            [pltpu.SemaphoreType.DMA((len(some),))],
            {len(some) + 1: 0} if held else None,
        )
    return result.reshape(ocean_state.shape)


def solution(mesh):
    placed = (
        P("member", None, "slab", None, None),
        P("member", None, "slab", None),
        P("member", "slab", None),
        P(None, None, "slab", "member"),
        P("member", None, None),
        P("member", None, None),
    )
    return jax.shard_map(
        functools.partial(per_device, mesh.shape["slab"]),
        mesh=mesh,
        in_specs=placed,
        out_specs=P("member", None, "slab", None, None),
        check_vma=False,
    )
```

```python
import functools

import jax
import jax.numpy as jnp
from jax import lax
from jax.experimental import pallas as pl
from jax.experimental.pallas import tpu as pltpu
from jax.sharding import PartitionSpec as P

STEPS = 2
COURANT = 0.2
F32 = jnp.float32


def shift_next(block, after):
    rows = block.shape[0]
    row_ids = lax.broadcasted_iota(jnp.int32, block.shape, 0)
    return jnp.where(row_ids == rows - 1, after, pltpu.roll(block, rows - 1, 0))


def shift_prev(block, before):
    row_ids = lax.broadcasted_iota(jnp.int32, block.shape, 0)
    return jnp.where(row_ids == 0, before, pltpu.roll(block, 1, 0))


def lane_next(block):
    return pltpu.roll(block, block.shape[1] - 1, 1)


def lane_prev(block):
    return pltpu.roll(block, 1, 1)


def advect_tile(tracers, zonal, merid, counts, level):
    cell_n, zonal_n, zonal_first_n, merid_n = counts
    u, u_before, u_after = zonal
    face_u = jnp.where(level < zonal_n, 0.25 * (u + shift_next(u, u_after)), 0.0)
    first_u = jnp.where(level < zonal_first_n, 0.25 * (u_before + u[0:1]), 0.0)
    face_v = jnp.where(level < merid_n, 0.25 * (merid + lane_next(merid)), 0.0)
    out = []
    for c, c_before, c_after in tracers:
        flux_x = face_u * (c + shift_next(c, c_after))
        first_x = first_u * (c_before + c[0:1])
        flux_y = face_v * (c + lane_next(c))
        spread = (flux_x - shift_prev(flux_x, first_x)) + (flux_y - lane_prev(flux_y))
        out.append(jnp.where(level < cell_n, c - COURANT * spread, 0.0))
    return out


def advect_kernel(groups, rows, scal, state, cell_n, zonal_n, merid_n, *outs):
    nx = state.shape[3]
    level = scal[2] + pl.program_id(1)
    for part in range(groups):
        for tile in range(2):
            row0 = (tile * groups + (scal[0] ^ part)) * rows
            before = pl.multiple_of(lax.rem(row0 + nx - 8, nx), 8)
            after = pl.multiple_of(lax.rem(row0 + rows, nx), 8)
            here = pl.multiple_of(row0, 8)

            def whole(field):
                return (
                    state[0, field, 0, pl.ds(here, rows), :],
                    state[0, field, 0, pl.ds(before, 8), :][7:8],
                    state[0, field, 0, pl.ds(after, 8), :][0:1],
                )

            counts = (
                cell_n[0, pl.ds(here, rows), :],
                zonal_n[0, pl.ds(here, rows), :],
                zonal_n[0, pl.ds(before, 8), :][7:8],
                merid_n[0, pl.ds(here, rows), :],
            )
            merid = state[0, 3, 0, pl.ds(here, rows), :]
            moved = advect_tile([whole(0), whole(1)], whole(2), merid, counts, level)
            for field in range(2):
                outs[part][0, field, 0, tile] = moved[field]


def split_kernel(groups, scal, state, *refs):
    outs, sem = refs[:groups], refs[groups]
    copies = [
        pltpu.make_async_copy(state.at[:, pl.ds(2, 2), :, :, scal[0] ^ part], outs[part], sem.at[part])
        for part in range(groups)
    ]
    for copy in copies:
        copy.start()
    for copy in copies:
        copy.wait()


def give_kernel(half_levels, scal, own, drag, land, bottom, out, mid_other):
    half = scal[1]
    count = jnp.where(land[0] == 1, bottom[0], 0)
    shape = count.shape
    for e in range(half_levels):
        out[0, e] = own[0, (1 - half) * (half_levels - 1) + e]
    out[0, half_levels] = drag[0]

    def ends(which):
        top = which == 0
        prev = jnp.zeros(shape, F32)
        c_t = prev
        c_v = prev
        for e in range(half_levels):
            upper = jnp.where(top, e, 2 * half_levels - 2 - e)
            level = jnp.where(top, e, 2 * half_levels - 1 - e)
            r = jnp.where(upper + 1 < count, own[0, upper], 0.0)
            base = 1.0 + r
            c_v = r / (base + prev * (1.0 - c_v) + jnp.where(level == count - 1, drag[0], 0.0))
            c_t = r / (base + prev * (1.0 - c_t))
            prev = r
        return c_t, c_v

    mine = ends(half)
    others = ends(1 - half)
    for kind in range(2):
        out[0, half_levels + 1 + kind] = mine[kind]
        mid_other[0, kind] = others[kind]


def factor_kernel(half_levels, scal, own, got, own_drag, own_other, cell_n, rate, inv_t, inv_v, mid, mid_other):
    half = scal[1]
    tile = pl.program_id(1)
    top = half == 0
    start = half * (half_levels - 1)
    is_own = tile == half
    count = cell_n[0, 0]
    shape = count.shape
    drag = jnp.where(is_own, own_drag[0], got[0, half_levels])
    prev = jnp.zeros(shape, F32)
    c_t = prev
    c_v = prev
    for e in range(half_levels):
        spot = jnp.where(top, e, half_levels - 1 - e)
        deeper = jnp.where(top, e + 1, 2 * half_levels - 1 - e)
        level = jnp.where(top, e, 2 * half_levels - 1 - e)
        diff = jnp.where(is_own, own[0, start + spot], got[0, spot])
        r = jnp.where(deeper < count, diff, 0.0)
        base = 1.0 + r
        den_t = base + prev * (1.0 - c_t)
        den_v = base + prev * (1.0 - c_v) + jnp.where(level == count - 1, drag, 0.0)
        i_t = 1.0 / den_t
        i_v = 1.0 / den_v
        rate[0, 0, e] = r
        inv_t[0, 0, e] = i_t
        inv_v[0, 0, e] = i_v
        c_t = r * i_t
        c_v = r * i_v
        prev = r
    mid[0, 0, 0] = c_t
    mid[0, 0, 1] = c_v
    for kind in range(2):
        mid_other[0, 0, kind] = jnp.where(is_own, own_other[0, kind], got[0, half_levels + 1 + kind])


def sweep(rhs, rate, inv, store):
    half_levels = rate.shape[2]
    carry = [None, None]
    before = None
    for e in range(half_levels):
        inverse = inv[0, 0, e]
        for f in range(2):
            value = rhs(e, f)
            if e > 0:
                value = value + before * carry[f]
            carry[f] = value * inverse
            store(e, f, carry[f])
        before = rate[0, 0, e]
    return carry


def back(d_ref, other, rate, inv, mid, mid_other, kind, store):
    half_levels = rate.shape[2]
    last = half_levels - 1
    c_own = mid[0, 0, kind]
    c_oth = mid_other[0, 0, kind]
    scale = 1.0 / (1.0 - c_own * c_oth)
    value = [(d_ref[0, 0, f, last] + c_own * other[0, 0, f]) * scale for f in range(2)]
    for f in range(2):
        store(last, f, value[f])
    for e in range(last - 1, -1, -1):
        c = rate[0, 0, e] * inv[0, 0, e]
        for f in range(2):
            value[f] = d_ref[0, 0, f, e] + c * value[f]
            store(e, f, value[f])


def forced(forcing, count, force_ids, f):
    if force_ids[f] is None:
        return 0.0
    return jnp.where(count > 0, forcing[0, force_ids[f], 0], 0.0)


def slot_of(scal, part, lev, levels_own, half_levels):
    spot = (scal[0] ^ part) * levels_own + lev
    return jnp.where(scal[1] == 0, spot, half_levels - 1 - spot)


def first_kernel(parts, levels_own, force_ids, masked, scal, *refs):
    groups = len(parts)
    chunks = refs[:groups]
    rate, inv, cell_n, forcing, d_ref, mid_ref, buf = refs[groups:]
    half_levels = rate.shape[2]
    count = cell_n[0, 0]
    for chunk, part in zip(chunks, parts):
        for lev in range(levels_own):
            slot = slot_of(scal, part, lev, levels_own, half_levels)
            level = scal[1] * half_levels + (scal[0] ^ part) * levels_own + lev
            for f in range(2):
                value = chunk[0, f, lev, 0]
                buf[f, slot] = value if masked else jnp.where(level < count, value, 0.0)

    def rhs(e, f):
        value = buf[f, e]
        return value + forced(forcing, count, force_ids, f) if e == 0 else value

    def store(e, f, value):
        d_ref[0, 0, f, e] = value

    carry = sweep(rhs, rate, inv, store)
    for f in range(2):
        mid_ref[0, 0, f] = carry[f]


def middle_v_kernel(scal, d_ref, other, rate, inv, mid, mid_other, cell_n, forcing, x_ref, top_ref, end_ref, d2_ref, mid2_ref):
    rows = x_ref.shape[4]

    def keep(e, f, value):
        x_ref[0, 0, f, e] = value
        if f == 0:
            top_ref[0, 0, pl.ds(e, 1), :] = value[0:1]
            end_ref[0, 0, pl.ds(e, 1), :] = value[rows - 1 : rows]

    back(d_ref, other, rate, inv, mid, mid_other, 1, keep)
    count = cell_n[0, 0]

    def rhs(e, f):
        value = x_ref[0, 0, f, e]
        return value + forced(forcing, count, (1, 2), f) if e == 0 else value

    def store(e, f, value):
        d2_ref[0, 0, f, e] = value

    carry = sweep(rhs, rate, inv, store)
    for f in range(2):
        mid2_ref[0, 0, f] = carry[f]


def middle_t_kernel(scal, d_ref, other, rate, inv, mid, mid_other, u_top, u_end, x_ref, top_ref, end_ref):
    rows = x_ref.shape[4]
    top_ref[0, 0, 2] = u_top[0, 0]
    end_ref[0, 0, 2] = u_end[0, 0]

    def keep(e, f, value):
        x_ref[0, 0, f, e] = value
        top_ref[0, 0, f, pl.ds(e, 1), :] = value[0:1]
        end_ref[0, 0, f, pl.ds(e, 1), :] = value[rows - 1 : rows]

    back(d_ref, other, rate, inv, mid, mid_other, 0, keep)


def second_t_kernel(scal, x_ref, v_ref, before, after, rate, inv, cell_n, zonal_n, first_n, merid_n, forcing, d_ref, mid_ref, buf):
    half_levels = rate.shape[2]
    top = scal[1] == 0
    count = cell_n[0, 0]
    counts = (count, zonal_n[0, 0], first_n[0, 0], merid_n[0, 0])
    for e in range(half_levels):
        level = jnp.where(top, e, 2 * half_levels - 1 - e)

        def edges(f):
            return before[0, 0, f, e : e + 1, :], after[0, 0, f, e : e + 1, :]

        tracers = [(x_ref[0, 0, f, e],) + edges(f) for f in range(2)]
        zonal = (v_ref[0, 0, 0, e],) + edges(2)
        moved = advect_tile(tracers, zonal, v_ref[0, 0, 1, e], counts, level)
        for f in range(2):
            buf[f, e] = moved[f]

    def rhs(e, f):
        value = buf[f, e]
        return value + forced(forcing, count, (0, None), f) if e == 0 else value

    def store(e, f, value):
        d_ref[0, 0, f, e] = value

    carry = sweep(rhs, rate, inv, store)
    for f in range(2):
        mid_ref[0, 0, f] = carry[f]


def last_kernel(groups, levels_own, kind, scal, d_ref, other, rate, inv, mid, mid_other, *refs):
    outs, buf = refs[:groups], refs[groups]
    half_levels = rate.shape[2]

    def keep(e, f, value):
        buf[f, e] = value

    back(d_ref, other, rate, inv, mid, mid_other, kind, keep)
    for part in range(groups):
        for lev in range(levels_own):
            slot = slot_of(scal, part, lev, levels_own, half_levels)
            for f in range(2):
                outs[part][0, f, lev, 0] = buf[f, slot]


def place_kernel(pieces, scal, *refs):
    chunks = refs[: len(pieces)]
    out, sem = refs[-2:]
    copies = []
    for index, (field, part) in enumerate(pieces):
        copies.append(
            pltpu.make_async_copy(
                chunks[index], out.at[:, pl.ds(field, 2), :, :, scal[0] ^ part], sem.at[index]
            )
        )
    for copy in copies:
        copy.start()
    for copy in copies:
        copy.wait()


def pick(values, which):
    out = values[0]
    for index in range(1, len(values)):
        out = jnp.where(which == index, values[index], out)
    return out


SPLIT_LIMIT = 40


def call(kernel, name, scal, grid, inputs, outputs, scratch=(), aliases=None, limit=40, weight=1 / 1024):
    def spec(block, index):
        if block is None:
            return pl.BlockSpec(memory_space=pl.ANY)
        if block == "VMEM":
            return pl.BlockSpec(memory_space=pltpu.VMEM)
        return pl.BlockSpec(block, index)

    bytes_moved = sum(a.size * 4 for a, b, _ in inputs if b is not None)
    for s, b, _ in outputs:
        size = 4
        for dim in s:
            size *= dim
        bytes_moved += size
    return pl.pallas_call(
        kernel,
        grid_spec=pltpu.PrefetchScalarGridSpec(
            num_scalar_prefetch=1,
            grid=grid,
            in_specs=[spec(b, i) for _, b, i in inputs],
            out_specs=[spec(b, i) for _, b, i in outputs],
            scratch_shapes=list(scratch),
        ),
        out_shape=[jax.ShapeDtypeStruct(s, F32) for s, _, _ in outputs],
        input_output_aliases=aliases or {},
        compiler_params=pltpu.CompilerParams(vmem_limit_bytes=limit * 1024 * 1024),
        cost_estimate=pl.CostEstimate(flops=0, bytes_accessed=int(bytes_moved * weight), transcendentals=0),
        name=name,
    )(scal, *[a for a, _, _ in inputs])


def per_device(slabs, ocean_state, diffusivity, bottom_drag, surface_forcing, land_sea, bottom_level):
    members, _, own, nx, ny = ocean_state.shape
    groups = slabs // 2
    rows = nx // slabs
    levels = diffusivity.shape[1]
    half_levels = levels // 2
    slab = lax.axis_index("slab")
    half = slab // groups
    group = slab % groups
    partner = [(i, (i + groups) % slabs) for i in range(slabs)]

    def swap(values):
        return lax.ppermute(values, "slab", partner)

    def cross(values, parts=range(1, groups)):
        def moved(part):
            return [(i, (i // groups) * groups + ((i % groups) ^ part)) for i in range(slabs)]

        return [values[0]] + [
            lax.ppermute(values[part], "slab", moved(part)) if part in parts else None for part in range(1, groups)
        ]

    to_next = [(i, (i // groups) * groups + (i % groups + 1) % groups) for i in range(slabs)]
    to_prev = [(b, a) for a, b in to_next]

    scal = jnp.stack([group, half, slab * own]).astype(jnp.int32)

    view = ocean_state.reshape(members, 4, own, 2, groups, rows, ny)
    chunk_all = (members, 2, own, 2, rows, ny)
    chunk_level = (1, 2, 1, 2, rows, ny)
    v_send = call(
        functools.partial(split_kernel, groups),
        "split",
        scal,
        (),
        [(pltpu.with_memory_space_constraint(view, pltpu.HBM), None, None)],
        [(chunk_all, "VMEM", None)] * groups,
        [pltpu.SemaphoreType.DMA((groups,))],
        limit=SPLIT_LIMIT,
    )
    f_got = swap(surface_forcing)
    v_send, (diffusivity, bottom_drag, land_sea, bottom_level, ocean_late) = lax.optimization_barrier(
        (v_send, (diffusivity, bottom_drag, land_sea, bottom_level, ocean_state))
    )
    v_got = cross(v_send)

    give, own_other = call(
        functools.partial(give_kernel, half_levels),
        "give",
        scal,
        (members,),
        [
            (diffusivity, (1, levels, rows, ny), lambda m, s: (m, 0, 0, 0)),
            (bottom_drag, (1, rows, ny), lambda m, s: (m, 0, 0)),
            (land_sea, (1, rows, ny), lambda m, s: (m, s[1] * groups + s[0], 0)),
            (bottom_level, (1, rows, ny), lambda m, s: (m, s[1] * groups + s[0], 0)),
        ],
        [
            ((members, half_levels + 3, rows, ny), (1, half_levels + 3, rows, ny), lambda m, s: (m, 0, 0, 0)),
            ((members, 2, rows, ny), (1, 2, rows, ny), lambda m, s: (m, 0, 0, 0)),
        ],
    )
    give, land_sea, bottom_level, ocean_late = lax.optimization_barrier((give, land_sea, bottom_level, ocean_late))
    got = swap(give)

    f_tiles = jnp.where(half == 0, jnp.stack([surface_forcing, f_got], axis=2), 0.0)
    places = lax.axis_size("member")
    place = lax.axis_index("member")
    f_parts = [f_tiles] + [
        lax.ppermute(f_tiles, "member", [(i, (i + step) % places) for i in range(places)]) for step in range(1, places)
    ]
    forcing = jnp.concatenate([pick(f_parts, lax.rem(place - q + places, places)) for q in range(places)], axis=4)

    cell_n = jnp.where(land_sea == 1, bottom_level, 0)
    zonal_n = jnp.minimum(cell_n, jnp.roll(cell_n, -1, axis=1))
    merid_n = jnp.minimum(cell_n, jnp.concatenate([cell_n[:, :, 1:], jnp.zeros_like(cell_n[:, :, :1])], axis=2))

    def tiles(values):
        return lax.dynamic_index_in_dim(values.reshape(members, 2, groups, rows, ny), group, 2, keepdims=False)

    cell_t = tiles(cell_n)
    zonal_t = tiles(zonal_n)
    merid_t = tiles(merid_n)
    first_t = tiles(jnp.roll(zonal_n, 1, axis=1))[:, :, :1]

    t_send = call(
        functools.partial(advect_kernel, groups, rows),
        "advect",
        scal,
        (members, own),
        [
            (pltpu.with_memory_space_constraint(ocean_late, pltpu.HBM), (1, 4, 1, nx, ny), lambda m, l, s: (m, 0, l, 0, 0)),
            (cell_n, (1, nx, ny), lambda m, l, s: (m, 0, 0)),
            (zonal_n, (1, nx, ny), lambda m, l, s: (m, 0, 0)),
            (merid_n, (1, nx, ny), lambda m, l, s: (m, 0, 0)),
        ],
        [(chunk_all, chunk_level, lambda m, l, s: (m, 0, l, 0, 0, 0))] * groups,
    )

    t_send = list(t_send)
    t_send[:-1], got, forcing = lax.optimization_barrier((t_send[:-1], got, forcing))
    t_got = cross(t_send, range(1, groups - 1))

    col_shape = (members, 2, half_levels, rows, ny)
    col_block = (1, 1, half_levels, rows, ny)
    mid_shape = (members, 2, 2, rows, ny)
    mid_block = (1, 1, 2, rows, ny)
    rate, inv_t, inv_v, mid, mid_other = call(
        functools.partial(factor_kernel, half_levels),
        "factor",
        scal,
        (members, 2),
        [
            (diffusivity, (1, levels, rows, ny), lambda m, t, s: (m, 0, 0, 0)),
            (got, (1, half_levels + 3, rows, ny), lambda m, t, s: (m, 0, 0, 0)),
            (pltpu.with_memory_space_constraint(bottom_drag, pltpu.HBM), (1, rows, ny), lambda m, t, s: (m, 0, 0)),
            (pltpu.with_memory_space_constraint(own_other, pltpu.HBM), (1, 2, rows, ny), lambda m, t, s: (m, 0, 0, 0)),
            (cell_t, (1, 1, rows, ny), lambda m, t, s: (m, t, 0, 0)),
        ],
        [
            (col_shape, col_block, lambda m, t, s: (m, t, 0, 0, 0)),
            (col_shape, col_block, lambda m, t, s: (m, t, 0, 0, 0)),
            (col_shape, col_block, lambda m, t, s: (m, t, 0, 0, 0)),
            (mid_shape, mid_block, lambda m, t, s: (m, t, 0, 0, 0)),
            (mid_shape, mid_block, lambda m, t, s: (m, t, 0, 0, 0)),
        ],
    )

    state_block = (1, 1, 2, half_levels, rows, ny)
    pair_block = (1, 1, 2, rows, ny)

    def at(m0):
        def mine(extra):
            return lambda m, t, s: (m, t) + (0,) * extra

        def shared(extra):
            return lambda m, t, s: (m + m0, t) + (0,) * extra

        return mine, shared

    def first(chunks, m0, count, inv, force_ids, masked, parts):
        mine, shared = at(m0)
        return call(
            functools.partial(first_kernel, tuple(parts), own, force_ids, masked),
            "first",
            scal,
            (count, 2),
            [(c, (1, 2, own, 1, rows, ny), lambda m, t, s: (m + m0, 0, 0, t, 0, 0)) for c in (chunks[p] for p in parts)]
            + [
                (rate, col_block, shared(3)),
                (inv, col_block, shared(3)),
                (cell_t, (1, 1, rows, ny), shared(2)),
                (forcing, (1, 3, 1, rows, ny), lambda m, t, s: (0, 0, t, 0, 0)),
            ],
            [
                ((count, 2, 2, half_levels, rows, ny), state_block, mine(4)),
                ((count, 2, 2, rows, ny), pair_block, mine(3)),
            ],
            [pltpu.VMEM((2, half_levels, rows, ny), F32)],
            weight=4,
        )

    def last(d, other, m0, count, inv, kind):
        mine, shared = at(m0)
        return call(
            functools.partial(last_kernel, groups, own, kind),
            "last",
            scal,
            (count, 2),
            [
                (d, state_block, mine(4)),
                (other, pair_block, mine(3)),
                (rate, col_block, shared(3)),
                (inv, col_block, shared(3)),
                (mid, pair_block, shared(3)),
                (mid_other, pair_block, shared(3)),
            ],
            [((count, 2, own, 2, rows, ny), (1, 2, own, 1, rows, ny), lambda m, t, s: (m, 0, 0, t, 0, 0))] * groups,
            [pltpu.VMEM((2, half_levels, rows, ny), F32)],
        )

    mine, shared = at(0)
    d_v, dm_v = first(v_got, 0, members, inv_v, (1, 2), False, [0, groups - 1] + list(range(1, groups - 1)))
    dm_v_other = swap(dm_v)
    t_send[-1], dm_v = lax.optimization_barrier((t_send[-1], dm_v))
    dm_v_other, t_got[1:-1] = lax.optimization_barrier((dm_v_other, t_got[1:-1]))
    t_got[-1] = cross(t_send, [groups - 1])[-1]
    d_t, dm_t = first(t_got, 0, members, inv_t, (0, None), True, range(groups))
    x_v, u_top, u_end, d2_v, dm2_v = call(
        middle_v_kernel,
        "middle_v",
        scal,
        (members, 2),
        [
            (d_v, state_block, mine(4)),
            (dm_v_other, pair_block, mine(3)),
            (rate, col_block, shared(3)),
            (inv_v, col_block, shared(3)),
            (mid, pair_block, shared(3)),
            (mid_other, pair_block, shared(3)),
            (cell_t, (1, 1, rows, ny), shared(2)),
            (forcing, (1, 3, 1, rows, ny), lambda m, t, s: (1, 0, t, 0, 0)),
        ],
        [
            ((members, 2, 2, half_levels, rows, ny), state_block, mine(4)),
            ((members, 2, half_levels, ny), (1, 1, half_levels, ny), mine(2)),
            ((members, 2, half_levels, ny), (1, 1, half_levels, ny), mine(2)),
            ((members, 2, 2, half_levels, rows, ny), state_block, mine(4)),
            ((members, 2, 2, rows, ny), pair_block, mine(3)),
        ],
        weight=2,
    )
    dm2_v_other = swap(dm2_v)
    out_v = last(d2_v, dm2_v_other, 0, members, inv_v, 1)
    out_v, dm_t = lax.optimization_barrier((list(out_v), dm_t))
    back_v = cross(out_v, range(1, groups - 1))

    back_t = []
    for m in range(1):
        dm_t_other = swap(dm_t)
        mine, shared = at(m)
        x_t, t_top, t_end = call(
            middle_t_kernel,
            "middle_t",
            scal,
            (members, 2),
            [
                (d_t, state_block, mine(4)),
                (dm_t_other, pair_block, mine(3)),
                (rate, col_block, shared(3)),
                (inv_t, col_block, shared(3)),
                (mid, pair_block, shared(3)),
                (mid_other, pair_block, shared(3)),
                (u_top, (1, 1, half_levels, ny), mine(2)),
                (u_end, (1, 1, half_levels, ny), mine(2)),
            ],
            [
                ((members, 2, 2, half_levels, rows, ny), state_block, mine(4)),
                ((members, 2, 3, half_levels, ny), (1, 1, 3, half_levels, ny), mine(3)),
                ((members, 2, 3, half_levels, ny), (1, 1, 3, half_levels, ny), mine(3)),
            ],
        )
        t_before = lax.ppermute(t_end, "slab", to_next)
        t_after = lax.ppermute(t_top, "slab", to_prev)
        out_v[-1], t_before, t_after = lax.optimization_barrier((out_v[-1], t_before, t_after))
        back_v[-1] = cross(out_v, [groups - 1])[-1]

        def from_before(extra, m0):
            return lambda i, t, s: (i + m0, t ^ jnp.where(s[0] == 0, 1, 0)) + (0,) * extra

        def from_after(extra, m0):
            return lambda i, t, s: (i + m0, t ^ jnp.where(s[0] == groups - 1, 1, 0)) + (0,) * extra

        x_t, back_v[1:-1] = lax.optimization_barrier((x_t, back_v[1:-1]))
        d2_t, dm2_t = call(
            second_t_kernel,
            "second_t",
            scal,
            (members, 2),
            [
                (x_t, state_block, mine(4)),
                (x_v, state_block, shared(4)),
                (t_before, (1, 1, 3, half_levels, ny), from_before(3, 0)),
                (t_after, (1, 1, 3, half_levels, ny), from_after(3, 0)),
                (rate, col_block, shared(3)),
                (inv_t, col_block, shared(3)),
                (cell_t, (1, 1, rows, ny), shared(2)),
                (zonal_t, (1, 1, rows, ny), shared(2)),
                (first_t, (1, 1, 1, ny), shared(2)),
                (merid_t, (1, 1, rows, ny), shared(2)),
                (forcing, (1, 3, 1, rows, ny), lambda i, t, s: (1, 0, t, 0, 0)),
            ],
            [
                ((members, 2, 2, half_levels, rows, ny), state_block, mine(4)),
                ((members, 2, 2, rows, ny), pair_block, mine(3)),
            ],
            [pltpu.VMEM((2, half_levels, rows, ny), F32)],
        )
        d2_t, back_v[-1] = lax.optimization_barrier((d2_t, back_v[-1]))
        back_t.append(cross(last(d2_t, swap(dm2_t), m, members, inv_t, 0)))

    whole = view.shape
    chunks = {(2, part): back_v[part] for part in range(groups)}
    chunks.update({(0, part): back_t[0][part] for part in range(groups)})
    pieces = list(chunks)
    result = None
    for some in (pieces[: groups + 1], pieces[groups + 1 : -1], pieces[-1:]):
        held = [] if result is None else [(result, None, None)]
        (result,) = call(
            functools.partial(place_kernel, some),
            "place",
            scal,
            (),
            [(chunks[piece], "VMEM", None) for piece in some] + held,
            [(whole, None, None)],
            [pltpu.SemaphoreType.DMA((len(some),))],
            {len(some) + 1: 0} if held else None,
        )
    return result.reshape(ocean_state.shape)


def solution(mesh):
    placed = (
        P("member", None, "slab", None, None),
        P("member", None, "slab", None),
        P("member", "slab", None),
        P(None, None, "slab", "member"),
        P("member", None, None),
        P("member", None, None),
    )
    return jax.shard_map(
        functools.partial(per_device, mesh.shape["slab"]),
        mesh=mesh,
        in_specs=placed,
        out_specs=P("member", None, "slab", None, None),
        check_vma=False,
    )
```

```python
import functools

import jax
import jax.numpy as jnp
from jax import lax
from jax.experimental import pallas as pl
from jax.experimental.pallas import tpu as pltpu
from jax.sharding import PartitionSpec as P

STEPS = 2
COURANT = 0.2
F32 = jnp.float32


def shift_next(block, after):
    rows = block.shape[0]
    row_ids = lax.broadcasted_iota(jnp.int32, block.shape, 0)
    return jnp.where(row_ids == rows - 1, after, pltpu.roll(block, rows - 1, 0))


def shift_prev(block, before):
    row_ids = lax.broadcasted_iota(jnp.int32, block.shape, 0)
    return jnp.where(row_ids == 0, before, pltpu.roll(block, 1, 0))


def lane_next(block):
    return pltpu.roll(block, block.shape[1] - 1, 1)


def lane_prev(block):
    return pltpu.roll(block, 1, 1)


def advect_tile(tracers, zonal, merid, counts, level):
    cell_n, zonal_n, zonal_first_n, merid_n = counts
    u, u_before, u_after = zonal
    face_u = jnp.where(level < zonal_n, 0.25 * (u + shift_next(u, u_after)), 0.0)
    first_u = jnp.where(level < zonal_first_n, 0.25 * (u_before + u[0:1]), 0.0)
    face_v = jnp.where(level < merid_n, 0.25 * (merid + lane_next(merid)), 0.0)
    out = []
    for c, c_before, c_after in tracers:
        flux_x = face_u * (c + shift_next(c, c_after))
        first_x = first_u * (c_before + c[0:1])
        flux_y = face_v * (c + lane_next(c))
        spread = (flux_x - shift_prev(flux_x, first_x)) + (flux_y - lane_prev(flux_y))
        out.append(jnp.where(level < cell_n, c - COURANT * spread, 0.0))
    return out


def advect_kernel(groups, rows, scal, state, cell_n, zonal_n, merid_n, *outs):
    nx = state.shape[3]
    level = scal[2] + pl.program_id(1)
    for part in range(groups):
        for tile in range(2):
            row0 = (tile * groups + (scal[0] ^ part)) * rows
            before = pl.multiple_of(lax.rem(row0 + nx - 8, nx), 8)
            after = pl.multiple_of(lax.rem(row0 + rows, nx), 8)
            here = pl.multiple_of(row0, 8)

            def whole(field):
                return (
                    state[0, field, 0, pl.ds(here, rows), :],
                    state[0, field, 0, pl.ds(before, 8), :][7:8],
                    state[0, field, 0, pl.ds(after, 8), :][0:1],
                )

            counts = (
                cell_n[0, pl.ds(here, rows), :],
                zonal_n[0, pl.ds(here, rows), :],
                zonal_n[0, pl.ds(before, 8), :][7:8],
                merid_n[0, pl.ds(here, rows), :],
            )
            merid = state[0, 3, 0, pl.ds(here, rows), :]
            moved = advect_tile([whole(0), whole(1)], whole(2), merid, counts, level)
            for field in range(2):
                outs[part][0, field, 0, tile] = moved[field]


def split_kernel(groups, scal, state, *refs):
    outs, sem = refs[:groups], refs[groups]
    copies = [
        pltpu.make_async_copy(state.at[:, pl.ds(2, 2), :, :, scal[0] ^ part], outs[part], sem.at[part])
        for part in range(groups)
    ]
    for copy in copies:
        copy.start()
    for copy in copies:
        copy.wait()


def give_kernel(half_levels, scal, own, drag, land, bottom, out, mid_other):
    half = scal[1]
    count = jnp.where(land[0] == 1, bottom[0], 0)
    shape = count.shape
    for e in range(half_levels):
        out[0, e] = own[0, (1 - half) * (half_levels - 1) + e]
    out[0, half_levels] = drag[0]

    def ends(which):
        top = which == 0
        prev = jnp.zeros(shape, F32)
        c_t = prev
        c_v = prev
        for e in range(half_levels):
            upper = jnp.where(top, e, 2 * half_levels - 2 - e)
            level = jnp.where(top, e, 2 * half_levels - 1 - e)
            r = jnp.where(upper + 1 < count, own[0, upper], 0.0)
            base = 1.0 + r
            c_v = r / (base + prev * (1.0 - c_v) + jnp.where(level == count - 1, drag[0], 0.0))
            c_t = r / (base + prev * (1.0 - c_t))
            prev = r
        return c_t, c_v

    mine = ends(half)
    others = ends(1 - half)
    for kind in range(2):
        out[0, half_levels + 1 + kind] = mine[kind]
        mid_other[0, kind] = others[kind]


def factor_kernel(half_levels, scal, own, got, own_drag, own_other, cell_n, rate, inv_t, inv_v, mid, mid_other):
    half = scal[1]
    tile = pl.program_id(1)
    top = half == 0
    start = half * (half_levels - 1)
    is_own = tile == half
    count = cell_n[0, 0]
    shape = count.shape
    drag = jnp.where(is_own, own_drag[0], got[0, half_levels])
    prev = jnp.zeros(shape, F32)
    c_t = prev
    c_v = prev
    for e in range(half_levels):
        spot = jnp.where(top, e, half_levels - 1 - e)
        deeper = jnp.where(top, e + 1, 2 * half_levels - 1 - e)
        level = jnp.where(top, e, 2 * half_levels - 1 - e)
        diff = jnp.where(is_own, own[0, start + spot], got[0, spot])
        r = jnp.where(deeper < count, diff, 0.0)
        base = 1.0 + r
        den_t = base + prev * (1.0 - c_t)
        den_v = base + prev * (1.0 - c_v) + jnp.where(level == count - 1, drag, 0.0)
        i_t = 1.0 / den_t
        i_v = 1.0 / den_v
        rate[0, 0, e] = r
        inv_t[0, 0, e] = i_t
        inv_v[0, 0, e] = i_v
        c_t = r * i_t
        c_v = r * i_v
        prev = r
    mid[0, 0, 0] = c_t
    mid[0, 0, 1] = c_v
    for kind in range(2):
        mid_other[0, 0, kind] = jnp.where(is_own, own_other[0, kind], got[0, half_levels + 1 + kind])


def sweep(rhs, rate, inv, store):
    half_levels = rate.shape[2]
    carry = [None, None]
    before = None
    for e in range(half_levels):
        inverse = inv[0, 0, e]
        for f in range(2):
            value = rhs(e, f)
            if e > 0:
                value = value + before * carry[f]
            carry[f] = value * inverse
            store(e, f, carry[f])
        before = rate[0, 0, e]
    return carry


def back(d_ref, other, rate, inv, mid, mid_other, kind, store):
    half_levels = rate.shape[2]
    last = half_levels - 1
    c_own = mid[0, 0, kind]
    c_oth = mid_other[0, 0, kind]
    scale = 1.0 / (1.0 - c_own * c_oth)
    value = [(d_ref[0, 0, f, last] + c_own * other[0, 0, f]) * scale for f in range(2)]
    for f in range(2):
        store(last, f, value[f])
    for e in range(last - 1, -1, -1):
        c = rate[0, 0, e] * inv[0, 0, e]
        for f in range(2):
            value[f] = d_ref[0, 0, f, e] + c * value[f]
            store(e, f, value[f])


def forced(forcing, count, force_ids, f):
    if force_ids[f] is None:
        return 0.0
    return jnp.where(count > 0, forcing[0, force_ids[f], 0], 0.0)


def slot_of(scal, part, lev, levels_own, half_levels):
    spot = (scal[0] ^ part) * levels_own + lev
    return jnp.where(scal[1] == 0, spot, half_levels - 1 - spot)


def first_kernel(parts, levels_own, force_ids, masked, scal, *refs):
    groups = len(parts)
    chunks = refs[:groups]
    rate, inv, cell_n, forcing, d_ref, mid_ref, buf = refs[groups:]
    half_levels = rate.shape[2]
    count = cell_n[0, 0]
    for chunk, part in zip(chunks, parts):
        for lev in range(levels_own):
            slot = slot_of(scal, part, lev, levels_own, half_levels)
            level = scal[1] * half_levels + (scal[0] ^ part) * levels_own + lev
            for f in range(2):
                value = chunk[0, f, lev, 0]
                buf[f, slot] = value if masked else jnp.where(level < count, value, 0.0)

    def rhs(e, f):
        value = buf[f, e]
        return value + forced(forcing, count, force_ids, f) if e == 0 else value

    def store(e, f, value):
        d_ref[0, 0, f, e] = value

    carry = sweep(rhs, rate, inv, store)
    for f in range(2):
        mid_ref[0, 0, f] = carry[f]


def middle_v_kernel(scal, d_ref, other, rate, inv, mid, mid_other, cell_n, forcing, x_ref, top_ref, end_ref, d2_ref, mid2_ref):
    rows = x_ref.shape[4]

    def keep(e, f, value):
        x_ref[0, 0, f, e] = value
        if f == 0:
            top_ref[0, 0, pl.ds(e, 1), :] = value[0:1]
            end_ref[0, 0, pl.ds(e, 1), :] = value[rows - 1 : rows]

    back(d_ref, other, rate, inv, mid, mid_other, 1, keep)
    count = cell_n[0, 0]

    def rhs(e, f):
        value = x_ref[0, 0, f, e]
        return value + forced(forcing, count, (1, 2), f) if e == 0 else value

    def store(e, f, value):
        d2_ref[0, 0, f, e] = value

    carry = sweep(rhs, rate, inv, store)
    for f in range(2):
        mid2_ref[0, 0, f] = carry[f]


def middle_t_kernel(scal, d_ref, other, rate, inv, mid, mid_other, u_top, u_end, x_ref, top_ref, end_ref):
    rows = x_ref.shape[4]
    top_ref[0, 0, 2] = u_top[0, 0]
    end_ref[0, 0, 2] = u_end[0, 0]

    def keep(e, f, value):
        x_ref[0, 0, f, e] = value
        top_ref[0, 0, f, pl.ds(e, 1), :] = value[0:1]
        end_ref[0, 0, f, pl.ds(e, 1), :] = value[rows - 1 : rows]

    back(d_ref, other, rate, inv, mid, mid_other, 0, keep)


def second_t_kernel(scal, x_ref, v_ref, before, after, rate, inv, cell_n, zonal_n, first_n, merid_n, forcing, d_ref, mid_ref, buf):
    half_levels = rate.shape[2]
    top = scal[1] == 0
    count = cell_n[0, 0]
    counts = (count, zonal_n[0, 0], first_n[0, 0], merid_n[0, 0])
    for e in range(half_levels):
        level = jnp.where(top, e, 2 * half_levels - 1 - e)

        def edges(f):
            return before[0, 0, f, e : e + 1, :], after[0, 0, f, e : e + 1, :]

        tracers = [(x_ref[0, 0, f, e],) + edges(f) for f in range(2)]
        zonal = (v_ref[0, 0, 0, e],) + edges(2)
        moved = advect_tile(tracers, zonal, v_ref[0, 0, 1, e], counts, level)
        for f in range(2):
            buf[f, e] = moved[f]

    def rhs(e, f):
        value = buf[f, e]
        return value + forced(forcing, count, (0, None), f) if e == 0 else value

    def store(e, f, value):
        d_ref[0, 0, f, e] = value

    carry = sweep(rhs, rate, inv, store)
    for f in range(2):
        mid_ref[0, 0, f] = carry[f]


def last_kernel(groups, levels_own, kind, scal, d_ref, other, rate, inv, mid, mid_other, *refs):
    outs, buf = refs[:groups], refs[groups]
    half_levels = rate.shape[2]

    def keep(e, f, value):
        buf[f, e] = value

    back(d_ref, other, rate, inv, mid, mid_other, kind, keep)
    for part in range(groups):
        for lev in range(levels_own):
            slot = slot_of(scal, part, lev, levels_own, half_levels)
            for f in range(2):
                outs[part][0, f, lev, 0] = buf[f, slot]


def place_kernel(pieces, scal, *refs):
    chunks = refs[: len(pieces)]
    out, sem = refs[-2:]
    copies = []
    for index, (field, part) in enumerate(pieces):
        copies.append(
            pltpu.make_async_copy(
                chunks[index], out.at[:, pl.ds(field, 2), :, :, scal[0] ^ part], sem.at[index]
            )
        )
    for copy in copies:
        copy.start()
    for copy in copies:
        copy.wait()


def pick(values, which):
    out = values[0]
    for index in range(1, len(values)):
        out = jnp.where(which == index, values[index], out)
    return out


SPLIT_LIMIT = 40


def call(kernel, name, scal, grid, inputs, outputs, scratch=(), aliases=None, limit=24, weight=1 / 1024):
    def spec(block, index):
        if block is None:
            return pl.BlockSpec(memory_space=pl.ANY)
        if block == "VMEM":
            return pl.BlockSpec(memory_space=pltpu.VMEM)
        return pl.BlockSpec(block, index)

    bytes_moved = sum(a.size * 4 for a, b, _ in inputs if b is not None)
    for s, b, _ in outputs:
        size = 4
        for dim in s:
            size *= dim
        bytes_moved += size
    return pl.pallas_call(
        kernel,
        grid_spec=pltpu.PrefetchScalarGridSpec(
            num_scalar_prefetch=1,
            grid=grid,
            in_specs=[spec(b, i) for _, b, i in inputs],
            out_specs=[spec(b, i) for _, b, i in outputs],
            scratch_shapes=list(scratch),
        ),
        out_shape=[jax.ShapeDtypeStruct(s, F32) for s, _, _ in outputs],
        input_output_aliases=aliases or {},
        compiler_params=pltpu.CompilerParams(vmem_limit_bytes=limit * 1024 * 1024),
        cost_estimate=pl.CostEstimate(flops=0, bytes_accessed=int(bytes_moved * weight), transcendentals=0),
        name=name,
    )(scal, *[a for a, _, _ in inputs])


def per_device(slabs, ocean_state, diffusivity, bottom_drag, surface_forcing, land_sea, bottom_level):
    members, _, own, nx, ny = ocean_state.shape
    groups = slabs // 2
    rows = nx // slabs
    levels = diffusivity.shape[1]
    half_levels = levels // 2
    slab = lax.axis_index("slab")
    half = slab // groups
    group = slab % groups
    partner = [(i, (i + groups) % slabs) for i in range(slabs)]

    def swap(values):
        return lax.ppermute(values, "slab", partner)

    def cross(values, parts=range(1, groups)):
        def moved(part):
            return [(i, (i // groups) * groups + ((i % groups) ^ part)) for i in range(slabs)]

        return [values[0]] + [
            lax.ppermute(values[part], "slab", moved(part)) if part in parts else None for part in range(1, groups)
        ]

    to_next = [(i, (i // groups) * groups + (i % groups + 1) % groups) for i in range(slabs)]
    to_prev = [(b, a) for a, b in to_next]

    scal = jnp.stack([group, half, slab * own]).astype(jnp.int32)

    view = ocean_state.reshape(members, 4, own, 2, groups, rows, ny)
    chunk_all = (members, 2, own, 2, rows, ny)
    chunk_level = (1, 2, 1, 2, rows, ny)
    v_send = call(
        functools.partial(split_kernel, groups),
        "split",
        scal,
        (),
        [(pltpu.with_memory_space_constraint(view, pltpu.HBM), None, None)],
        [(chunk_all, "VMEM", None)] * groups,
        [pltpu.SemaphoreType.DMA((groups,))],
        limit=SPLIT_LIMIT,
    )
    f_got = swap(surface_forcing)
    v_send, (diffusivity, bottom_drag, land_sea, bottom_level, ocean_late) = lax.optimization_barrier(
        (v_send, (diffusivity, bottom_drag, land_sea, bottom_level, ocean_state))
    )
    v_got = cross(v_send)

    give, own_other = call(
        functools.partial(give_kernel, half_levels),
        "give",
        scal,
        (members,),
        [
            (diffusivity, (1, levels, rows, ny), lambda m, s: (m, 0, 0, 0)),
            (bottom_drag, (1, rows, ny), lambda m, s: (m, 0, 0)),
            (land_sea, (1, rows, ny), lambda m, s: (m, s[1] * groups + s[0], 0)),
            (bottom_level, (1, rows, ny), lambda m, s: (m, s[1] * groups + s[0], 0)),
        ],
        [
            ((members, half_levels + 3, rows, ny), (1, half_levels + 3, rows, ny), lambda m, s: (m, 0, 0, 0)),
            ((members, 2, rows, ny), (1, 2, rows, ny), lambda m, s: (m, 0, 0, 0)),
        ],
    )
    give, land_sea, bottom_level, ocean_late = lax.optimization_barrier((give, land_sea, bottom_level, ocean_late))
    got = swap(give)

    f_tiles = jnp.where(half == 0, jnp.stack([surface_forcing, f_got], axis=2), 0.0)
    places = lax.axis_size("member")
    place = lax.axis_index("member")
    f_parts = [f_tiles] + [
        lax.ppermute(f_tiles, "member", [(i, (i + step) % places) for i in range(places)]) for step in range(1, places)
    ]
    forcing = jnp.concatenate([pick(f_parts, lax.rem(place - q + places, places)) for q in range(places)], axis=4)

    cell_n = jnp.where(land_sea == 1, bottom_level, 0)
    zonal_n = jnp.minimum(cell_n, jnp.roll(cell_n, -1, axis=1))
    merid_n = jnp.minimum(cell_n, jnp.concatenate([cell_n[:, :, 1:], jnp.zeros_like(cell_n[:, :, :1])], axis=2))

    def tiles(values):
        return lax.dynamic_index_in_dim(values.reshape(members, 2, groups, rows, ny), group, 2, keepdims=False)

    cell_t = tiles(cell_n)
    zonal_t = tiles(zonal_n)
    merid_t = tiles(merid_n)
    first_t = tiles(jnp.roll(zonal_n, 1, axis=1))[:, :, :1]

    t_send = call(
        functools.partial(advect_kernel, groups, rows),
        "advect",
        scal,
        (members, own),
        [
            (ocean_late, (1, 4, 1, nx, ny), lambda m, l, s: (m, 0, l, 0, 0)),
            (cell_n, (1, nx, ny), lambda m, l, s: (m, 0, 0)),
            (zonal_n, (1, nx, ny), lambda m, l, s: (m, 0, 0)),
            (merid_n, (1, nx, ny), lambda m, l, s: (m, 0, 0)),
        ],
        [(chunk_all, chunk_level, lambda m, l, s: (m, 0, l, 0, 0, 0))] * groups,
    )

    t_send = list(t_send)
    t_send[:-1], got, forcing = lax.optimization_barrier((t_send[:-1], got, forcing))
    t_got = cross(t_send, range(1, groups - 1))

    col_shape = (members, 2, half_levels, rows, ny)
    col_block = (1, 1, half_levels, rows, ny)
    mid_shape = (members, 2, 2, rows, ny)
    mid_block = (1, 1, 2, rows, ny)
    rate, inv_t, inv_v, mid, mid_other = call(
        functools.partial(factor_kernel, half_levels),
        "factor",
        scal,
        (members, 2),
        [
            (diffusivity, (1, levels, rows, ny), lambda m, t, s: (m, 0, 0, 0)),
            (got, (1, half_levels + 3, rows, ny), lambda m, t, s: (m, 0, 0, 0)),
            (pltpu.with_memory_space_constraint(bottom_drag, pltpu.HBM), (1, rows, ny), lambda m, t, s: (m, 0, 0)),
            (pltpu.with_memory_space_constraint(own_other, pltpu.HBM), (1, 2, rows, ny), lambda m, t, s: (m, 0, 0, 0)),
            (cell_t, (1, 1, rows, ny), lambda m, t, s: (m, t, 0, 0)),
        ],
        [
            (col_shape, col_block, lambda m, t, s: (m, t, 0, 0, 0)),
            (col_shape, col_block, lambda m, t, s: (m, t, 0, 0, 0)),
            (col_shape, col_block, lambda m, t, s: (m, t, 0, 0, 0)),
            (mid_shape, mid_block, lambda m, t, s: (m, t, 0, 0, 0)),
            (mid_shape, mid_block, lambda m, t, s: (m, t, 0, 0, 0)),
        ],
    )

    state_block = (1, 1, 2, half_levels, rows, ny)
    pair_block = (1, 1, 2, rows, ny)

    def at(m0):
        def mine(extra):
            return lambda m, t, s: (m, t) + (0,) * extra

        def shared(extra):
            return lambda m, t, s: (m + m0, t) + (0,) * extra

        return mine, shared

    def first(chunks, m0, count, inv, force_ids, masked, parts):
        mine, shared = at(m0)
        return call(
            functools.partial(first_kernel, tuple(parts), own, force_ids, masked),
            "first",
            scal,
            (count, 2),
            [(c, (1, 2, own, 1, rows, ny), lambda m, t, s: (m + m0, 0, 0, t, 0, 0)) for c in (chunks[p] for p in parts)]
            + [
                (rate, col_block, shared(3)),
                (inv, col_block, shared(3)),
                (cell_t, (1, 1, rows, ny), shared(2)),
                (forcing, (1, 3, 1, rows, ny), lambda m, t, s: (0, 0, t, 0, 0)),
            ],
            [
                ((count, 2, 2, half_levels, rows, ny), state_block, mine(4)),
                ((count, 2, 2, rows, ny), pair_block, mine(3)),
            ],
            [pltpu.VMEM((2, half_levels, rows, ny), F32)],
            weight=4,
        )

    def last(d, other, m0, count, inv, kind):
        mine, shared = at(m0)
        return call(
            functools.partial(last_kernel, groups, own, kind),
            "last",
            scal,
            (count, 2),
            [
                (d, state_block, mine(4)),
                (other, pair_block, mine(3)),
                (rate, col_block, shared(3)),
                (inv, col_block, shared(3)),
                (mid, pair_block, shared(3)),
                (mid_other, pair_block, shared(3)),
            ],
            [((count, 2, own, 2, rows, ny), (1, 2, own, 1, rows, ny), lambda m, t, s: (m, 0, 0, t, 0, 0))] * groups,
            [pltpu.VMEM((2, half_levels, rows, ny), F32)],
        )

    mine, shared = at(0)
    d_v, dm_v = first(v_got, 0, members, inv_v, (1, 2), False, [0, groups - 1] + list(range(1, groups - 1)))
    dm_v_other = swap(dm_v)
    t_send[-1], dm_v = lax.optimization_barrier((t_send[-1], dm_v))
    dm_v_other, t_got[1:-1] = lax.optimization_barrier((dm_v_other, t_got[1:-1]))
    t_got[-1] = cross(t_send, [groups - 1])[-1]
    d_t, dm_t = first(t_got, 0, members, inv_t, (0, None), True, range(groups))
    x_v, u_top, u_end, d2_v, dm2_v = call(
        middle_v_kernel,
        "middle_v",
        scal,
        (members, 2),
        [
            (d_v, state_block, mine(4)),
            (dm_v_other, pair_block, mine(3)),
            (rate, col_block, shared(3)),
            (inv_v, col_block, shared(3)),
            (mid, pair_block, shared(3)),
            (mid_other, pair_block, shared(3)),
            (cell_t, (1, 1, rows, ny), shared(2)),
            (forcing, (1, 3, 1, rows, ny), lambda m, t, s: (1, 0, t, 0, 0)),
        ],
        [
            ((members, 2, 2, half_levels, rows, ny), state_block, mine(4)),
            ((members, 2, half_levels, ny), (1, 1, half_levels, ny), mine(2)),
            ((members, 2, half_levels, ny), (1, 1, half_levels, ny), mine(2)),
            ((members, 2, 2, half_levels, rows, ny), state_block, mine(4)),
            ((members, 2, 2, rows, ny), pair_block, mine(3)),
        ],
        weight=2,
    )
    dm2_v_other = swap(dm2_v)
    out_v = last(d2_v, dm2_v_other, 0, members, inv_v, 1)
    out_v, dm_t = lax.optimization_barrier((list(out_v), dm_t))
    back_v = cross(out_v, range(1, groups - 1))

    back_t = []
    for m in range(1):
        dm_t_other = swap(dm_t)
        mine, shared = at(m)
        x_t, t_top, t_end = call(
            middle_t_kernel,
            "middle_t",
            scal,
            (members, 2),
            [
                (d_t, state_block, mine(4)),
                (dm_t_other, pair_block, mine(3)),
                (rate, col_block, shared(3)),
                (inv_t, col_block, shared(3)),
                (mid, pair_block, shared(3)),
                (mid_other, pair_block, shared(3)),
                (u_top, (1, 1, half_levels, ny), mine(2)),
                (u_end, (1, 1, half_levels, ny), mine(2)),
            ],
            [
                ((members, 2, 2, half_levels, rows, ny), state_block, mine(4)),
                ((members, 2, 3, half_levels, ny), (1, 1, 3, half_levels, ny), mine(3)),
                ((members, 2, 3, half_levels, ny), (1, 1, 3, half_levels, ny), mine(3)),
            ],
        )
        t_before = lax.ppermute(t_end, "slab", to_next)
        t_after = lax.ppermute(t_top, "slab", to_prev)
        out_v[-1], t_before, t_after = lax.optimization_barrier((out_v[-1], t_before, t_after))
        back_v[-1] = cross(out_v, [groups - 1])[-1]

        def from_before(extra, m0):
            return lambda i, t, s: (i + m0, t ^ jnp.where(s[0] == 0, 1, 0)) + (0,) * extra

        def from_after(extra, m0):
            return lambda i, t, s: (i + m0, t ^ jnp.where(s[0] == groups - 1, 1, 0)) + (0,) * extra

        x_t, back_v[1:-1] = lax.optimization_barrier((x_t, back_v[1:-1]))
        d2_t, dm2_t = call(
            second_t_kernel,
            "second_t",
            scal,
            (members, 2),
            [
                (x_t, state_block, mine(4)),
                (x_v, state_block, shared(4)),
                (t_before, (1, 1, 3, half_levels, ny), from_before(3, 0)),
                (t_after, (1, 1, 3, half_levels, ny), from_after(3, 0)),
                (rate, col_block, shared(3)),
                (inv_t, col_block, shared(3)),
                (cell_t, (1, 1, rows, ny), shared(2)),
                (zonal_t, (1, 1, rows, ny), shared(2)),
                (first_t, (1, 1, 1, ny), shared(2)),
                (merid_t, (1, 1, rows, ny), shared(2)),
                (forcing, (1, 3, 1, rows, ny), lambda i, t, s: (1, 0, t, 0, 0)),
            ],
            [
                ((members, 2, 2, half_levels, rows, ny), state_block, mine(4)),
                ((members, 2, 2, rows, ny), pair_block, mine(3)),
            ],
            [pltpu.VMEM((2, half_levels, rows, ny), F32)],
        )
        d2_t, back_v[-1] = lax.optimization_barrier((d2_t, back_v[-1]))
        back_t.append(cross(last(d2_t, swap(dm2_t), m, members, inv_t, 0)))

    whole = view.shape
    chunks = {(2, part): back_v[part] for part in range(groups)}
    chunks.update({(0, part): back_t[0][part] for part in range(groups)})
    pieces = list(chunks)
    result = None
    for some in (pieces[: groups + 1], pieces[groups + 1 : -1], pieces[-1:]):
        held = [] if result is None else [(result, None, None)]
        (result,) = call(
            functools.partial(place_kernel, some),
            "place",
            scal,
            (),
            [(chunks[piece], "VMEM", None) for piece in some] + held,
            [(whole, None, None)],
            [pltpu.SemaphoreType.DMA((len(some),))],
            {len(some) + 1: 0} if held else None,
        )
    return result.reshape(ocean_state.shape)


def solution(mesh):
    placed = (
        P("member", None, "slab", None, None),
        P("member", None, "slab", None),
        P("member", "slab", None),
        P(None, None, "slab", "member"),
        P("member", None, None),
        P("member", None, None),
    )
    return jax.shard_map(
        functools.partial(per_device, mesh.shape["slab"]),
        mesh=mesh,
        in_specs=placed,
        out_specs=P("member", None, "slab", None, None),
        check_vma=False,
    )
```
